32 devices in a mesh: groups: 2 (over x), dp: 2 (over core), ctx: 8 (over z, y).
Axes of the slice: x: 2, y: 2, z: 4, core: 2. Of those that a mesh axis runs over, the one named last changes fastest.
Arguments:
- h_fwd: bfloat16 [4, 1024, 1024], P(('groups', 'dp'), 'ctx'), parts along dimension 0, may hold values from -6 to 6
- h_rc: bfloat16 [4, 1024, 1024], P(('groups', 'dp'), 'ctx'), parts along dimension 0, may hold values from -6 to 6
- tokens: int32 [4, 1024], P(('groups', 'dp'), 'ctx'), parts along dimension 0, may hold values from 0 to 4
- loss_mask: int32 [4, 1024], P(('groups', 'dp'), 'ctx'), parts along dimension 0, may hold values from 0 to 1
- species: int32 [4], P(('groups', 'dp')), parts along dimension 0, may hold values from 0 to 7, as said below
- w_in: bfloat16 [1024, 2192], replicated, may hold values from -0.1875 to 0.1875
- a_log: float32 [16], replicated, may hold values from -6 to 0.5
- dt_bias: float32 [16], replicated, may hold values from -7 to 1
- d_skip: float32 [16], replicated, may hold values from 0.5 to 1.5
- norm_gain: float32 [1024], replicated, may hold values from 0.5 to 1.5
- w_out: bfloat16 [1024, 1024], replicated, may hold values from -0.1875 to 0.1875
- final_gain: float32 [1024], replicated, may hold values from 0.5 to 1.5
- w_head: float32 [5, 1024], replicated, may hold values from -0.5 to 0.5
- log_var: float32 [8], replicated, may hold values from -1 to 1
Outputs:
- loss: float32 [2], P('groups'), parts along dimension 0
- grad_log_var: float32 [16], P('groups'), parts along dimension 0
- grad_h_fwd: bfloat16 [4, 1024, 1024], P(('groups', 'dp'), 'ctx'), parts along dimension 0
- grad_h_rc: bfloat16 [4, 1024, 1024], P(('groups', 'dp'), 'ctx'), parts along dimension 0
- grad_w_in: float32 [2048, 2192], P(('groups', 'dp', 'ctx')), parts along dimension 0
- grad_w_out: float32 [2048, 1024], P(('groups', 'dp', 'ctx')), parts along dimension 0
The draws below stay inside these ranges and needn't reach their ends.
There are 2 independent parts, one for each index of `groups`. The reference program is written for one: setup_inputs(seed, part) draws one part's arguments, and reference() takes and returns one part's arrays. A program takes and returns all parts, laid end to end along the dimension named above; an argument that names none is the same for every part. Nothing has to cross between parts.
Inputs may be any that keep to these rules, and one draw needn't show every extreme that they name: Neighbouring sequences of one part belong to different species.
All inputs are finite; a program needn't handle non-finite values.
Results may differ from the reference program's by a relative error of at most 0.012.
The reference program's roundings to bfloat16 on the way count: a program that leaves them out, or rounds other values in their place, can miss the bound.
Values may be sent and summed in bfloat16 or wider, within the bound.
No kernel may reach another device: no remote copies, remote signals or barrier semaphores. Data moves between devices by JAX's collectives and lax.ppermute only.
A program may use at most 256 MiB of HBM per device.

```python
import jax
import jax.numpy as jnp
from jax import lax

D = 1024
HEADS = 16
HEAD_DIM = 64
STATE = 64
VOCAB = 5
SPECIES = 8
SPAN = 128
E = 1024
F = 2192
SEQS = 2
SEQ_LEN = 1024
N_CTX = 8


def decay_plan(key):
    base = jax.random.fold_in(key, 31)
    pick_key, slow_key, fast_key = jax.random.split(base, 3)
    threshold = 4
    slow_head = jax.random.randint(pick_key, (HEADS,), 0, 8) < threshold
    slow_window = 2.0 * SEQ_LEN * jax.random.uniform(slow_key, (HEADS,), jnp.float32, 1.0, 2.0)
    fast_window = jnp.maximum(0.16 * SPAN * jax.random.uniform(fast_key, (HEADS,), jnp.float32, 0.75, 1.25), 1.0)
    window = jnp.where(slow_head, slow_window, fast_window)
    return (window, lax.rsqrt(window))


def draw_a_log(key, part):
    window, step_mean = decay_plan(key)
    return (-0.5 * jnp.log(window)).astype(jnp.float32)


def draw_dt_bias(key, part):
    window, step_mean = decay_plan(key)
    return jnp.log(jnp.expm1(step_mean)).astype(jnp.float32)


def draw_loss_mask(key, part):
    mask_key = jax.random.fold_in(key, 57)
    positions = jnp.arange(SEQ_LEN, dtype=jnp.int32)
    limit = 100 + 200 * positions // SEQ_LEN
    rolls = jax.random.randint(mask_key, (SEQS, SEQ_LEN), 0, 1000)
    return (rolls < limit[None, :]).astype(jnp.int32)


def draw_species(key, part):
    order_key = jax.random.fold_in(key, 73)
    order = jax.random.permutation(order_key, jnp.arange(SPECIES, dtype=jnp.int32))
    picks = jnp.arange(SEQS, dtype=jnp.int32) % SPECIES
    return order[picks].astype(jnp.int32)


def place_ends(entries, stream_key, smallest, high):
    extent = entries.shape
    place = [jax.random.randint(jax.random.fold_in(stream_key, axis), (), 0, extent[axis]) for axis in range(len(extent))]
    entries = entries.at[tuple(place)].set(smallest)
    longest = extent.index(max(extent))
    place[longest] = (place[longest] + 1) % extent[longest]
    return entries.at[tuple(place)].set(high)


def with_spikes(drawn, own_key, source, target, blocks, factor):
    owner, partner = [(jnp.arange(drawn.shape[dim]) // (drawn.shape[dim] // blocks)).reshape([-1 if axis == dim else 1 for axis in range(drawn.ndim)]) for dim in (source, target)]
    chosen = jax.random.permutation(own_key, blocks)[partner]
    strong = (owner == chosen) | (owner == (partner + blocks // 2) % blocks)
    return jnp.where(strong, factor * drawn, drawn)


def steps_of(rng, extent, cuts, smallest, largest):
    level = 1.0
    for position, shards_of in cuts:
        draws = jax.random.uniform(jax.random.fold_in(jax.random.fold_in(rng, 6), position), (shards_of,), jnp.float32, smallest / len(cuts), largest / len(cuts))
        level = level * jnp.repeat(jnp.exp(draws), extent[position] // shards_of).reshape((-1,) + (1,) * (len(extent) - 1 - position))
    return level


def noise(own_key, shape, scale, most, shards=(), held_as=jnp.bfloat16):
    entries = jax.random.normal(own_key, shape, jnp.float32) * scale
    if len(shards) > 0:
        entries = steps_of(own_key, shape, shards, -0.22, 0.18) * entries
    return jnp.clip(entries, min=-most, max=most).astype(held_as)


def bell_draw_with(key, extent, scale, most, pieces, heavy, kind=jnp.bfloat16):
    drawn = scale * jax.random.normal(key, extent, jnp.float32)
    if pieces:
        drawn = drawn * steps_of(key, extent, pieces, -0.22, 0.18)
    return jnp.clip(with_spikes(drawn, jax.random.fold_in(key, 3), *heavy), -most, most).astype(kind)


def setup_inputs(seed: int = 0, part: int = 0) -> dict:
    key_of = jax.random.split(jax.random.key(seed), 15)
    part_keys = jax.random.split(jax.random.fold_in(key_of[14], part), 15)
    return {
        "h_fwd": bell_draw_with(part_keys[0], (SEQS, SEQ_LEN, D), 1.0, 6.0, ((0, 2), (1, 8)), (1, 2, 8, 2.0)),
        "h_rc": noise(part_keys[1], (SEQS, SEQ_LEN, D), 1.0, 6.0, ((0, 2), (1, 8))),
        "tokens": place_ends(jax.random.randint(part_keys[2], (SEQS, SEQ_LEN), 0, 5), jax.random.fold_in(part_keys[2], 1), 0, 4).astype(jnp.int32),
        "loss_mask": draw_loss_mask(jax.random.fold_in(jax.random.fold_in(key_of[14], part), 71), part),
        "species": draw_species(jax.random.fold_in(jax.random.fold_in(key_of[14], part), 71), part),
        "w_in": noise(key_of[5], (D, F), D ** -0.5, 0.1875),
        "a_log": draw_a_log(jax.random.fold_in(key_of[14], 71), part),
        "dt_bias": draw_dt_bias(jax.random.fold_in(key_of[14], 71), part),
        "d_skip": jnp.clip(jax.random.uniform(key_of[8], (HEADS,), jnp.float32, 0.5, 1.5), 0.5, 1.5),
        "norm_gain": jnp.clip(1.0 + 0.1 * jax.random.normal(key_of[9], (E,), jnp.float32), 0.5, 1.5),
        "w_out": noise(key_of[10], (E, D), E ** -0.5, 0.1875),
        "final_gain": jnp.clip(1.0 + 0.1 * jax.random.normal(key_of[11], (D,), jnp.float32), 0.5, 1.5),
        "w_head": noise(key_of[12], (VOCAB, D), (D // 9) ** -0.5, 0.5, (), jnp.float32),
        "log_var": jnp.clip(jax.random.uniform(key_of[13], (SPECIES,), jnp.float32, -1.0, 1.0), -1.0, 1.0),
    }


PRECISE = lax.Precision.HIGHEST
EPSILON = 1e-05
MASKED = -1e+30

def prepare(proj_f32, dt_bias, a_log):
    inner_width = HEADS * HEAD_DIM
    batch_rows, length = (proj_f32.shape[0], proj_f32.shape[1])
    values = proj_f32[..., :inner_width].reshape(batch_rows, length, HEADS, HEAD_DIM)
    gate_in = proj_f32[..., inner_width:2 * inner_width]
    keys_in = proj_f32[..., 2 * inner_width:2 * inner_width + STATE]
    read_vec = proj_f32[..., 2 * inner_width + STATE:2 * inner_width + 2 * STATE]
    step_size = jax.nn.softplus(proj_f32[..., 2 * inner_width + 2 * STATE:] + dt_bias)
    logdec = -jnp.exp(a_log) * step_size
    return (values, gate_in, keys_in, read_vec, step_size, logdec)

def summary(values, step_size, logdec, keys_in):
    cumulative = jnp.cumsum(logdec, axis=1)
    final_log = cumulative[:, -1]
    weights = jnp.exp(final_log[:, None] - cumulative) * step_size
    end_state = jnp.einsum('gth,gthp,gtn->ghpn', weights, values, keys_in, precision=PRECISE)
    return (jnp.exp(final_log), end_state)

def local_out(values, step_size, logdec, keys_in, read_vec, carry_in, d_skip):
    cumulative = jnp.cumsum(logdec, axis=1)
    length = values.shape[1]
    scores = jnp.einsum('gtn,gsn->gts', read_vec, keys_in, precision=PRECISE)
    lower_tri = lax.broadcasted_iota(jnp.int32, (length, length), 0) >= lax.broadcasted_iota(jnp.int32, (length, length), 1)
    cum_heads = jnp.swapaxes(cumulative, 1, 2)
    step_heads = jnp.swapaxes(step_size, 1, 2)
    segment = cum_heads[:, :, :, None] - cum_heads[:, :, None, :]
    segment = jnp.where(lower_tri[None, None, :, :], segment, MASKED)
    mixing = jnp.exp(segment) * scores[:, None, :, :] * step_heads[:, :, None, :]
    output = jnp.einsum('ghts,gshp->gthp', mixing, values, precision=PRECISE)
    output = output + jnp.einsum('gth,gtn,ghpn->gthp', jnp.exp(cumulative), read_vec, carry_in, precision=PRECISE)
    return output + d_skip[:, None] * values

def tail_mid(out_left, out_right, gate_in, norm_gain):

    def gated_norm(direction_out):
        gated_flat = direction_out.reshape(gate_in.shape) * jax.nn.silu(gate_in)
        return gated_flat * lax.rsqrt(lax.optimization_barrier(jnp.mean(gated_flat * gated_flat, axis=-1, keepdims=True)) + EPSILON) * norm_gain
    return gated_norm(out_left) + gated_norm(out_right)

def head_fn(mixed_in, hidden_in, final_gain, w_head):
    residual = hidden_in + mixed_in
    normed = residual * lax.rsqrt(lax.optimization_barrier(jnp.mean(residual * residual, axis=-1, keepdims=True)) + EPSILON) * final_gain
    return jnp.einsum('gtd,vd->gtv', normed, w_head, precision=PRECISE)

def complement(logits):
    return jnp.concatenate([logits[..., 3::-1], logits[..., 4:]], axis=-1)

def to_blocks(array):
    shaped = array.reshape((array.shape[0], N_CTX, SPAN) + array.shape[2:])
    return jnp.swapaxes(shaped, 0, 1)

def from_blocks(array):
    shaped = jnp.swapaxes(array, 0, 1)
    return shaped.reshape((shaped.shape[0], N_CTX * SPAN) + shaped.shape[3:])

def chain_states(blocked):
    decay_all, state_all = jax.vmap(summary)(*blocked)

    def advance(carry, member):
        decay_one, state_one = member
        return (decay_one[..., None, None] * carry + state_one, carry)
    unused, carries = lax.scan(advance, jnp.zeros_like(state_all[0]), (decay_all, state_all))
    return (decay_all, carries)

def run_direction(inputs, d_skip):
    blocked = tuple((to_blocks(member) for member in inputs))
    decay_all, carries = chain_states(blocked[:4])

    def local_apply(member):
        return local_out(member[0], member[1], member[2], member[3], member[4], member[5], d_skip)
    return from_blocks(lax.map(local_apply, blocked + (carries,)))

def grad_direction(inputs, d_out, d_skip):
    blocked = tuple((to_blocks(member) for member in inputs))
    decay_all, carries = chain_states(blocked[:4])

    def local_pull(member):

        def local_fn(values, step_size, logdec, keys_in, read_vec, carry_in):
            return local_out(values, step_size, logdec, keys_in, read_vec, carry_in, d_skip)
        unused, pull = jax.vjp(local_fn, *member[:6])
        return pull(member[6])
    local_grads = lax.map(local_pull, blocked + (carries, to_blocks(d_out)))
    direct = local_grads[5]

    def retreat(carry, member):
        decay_one, direct_one = member
        return (direct_one + decay_one[..., None, None] * carry, carry)
    unused, next_grads = lax.scan(retreat, jnp.zeros_like(direct[0]), (decay_all, direct), reverse=True)

    def summary_pull(member):
        unused_out, pull = jax.vjp(summary, *member[:4])
        return pull((lax.optimization_barrier(jnp.sum(member[4] * member[5], axis=(-2, -1))), member[4]))
    summary_grads = lax.map(summary_pull, blocked[:4] + (next_grads, carries))
    merged = (local_grads[0] + summary_grads[0], local_grads[1] + summary_grads[1], local_grads[2] + summary_grads[2], local_grads[3] + summary_grads[3], local_grads[4])
    return tuple((from_blocks(member) for member in merged))

def reference(h_fwd, h_rc, tokens, loss_mask, species, w_in, a_log, dt_bias, d_skip, norm_gain, w_out, final_gain, w_head, log_var):
    hidden = jnp.concatenate([h_fwd, h_rc[:, ::-1]], axis=0)
    batch_rows = hidden.shape[0]
    hidden_flat = hidden.reshape(batch_rows * SEQ_LEN, D)
    proj_b = jnp.dot(hidden_flat, w_in, preferred_element_type=jnp.float32).astype(jnp.bfloat16)
    proj_f32 = proj_b.astype(jnp.float32).reshape(batch_rows, SEQ_LEN, F)

    def prepare_local(proj_in):
        return prepare(proj_in, dt_bias, a_log)
    prepared, prep_pull = jax.vjp(prepare_local, proj_f32)
    values, gate_in, keys_in, read_vec, step_size, logdec = prepared
    left_in = (values, step_size, logdec, keys_in, read_vec)
    right_in = tuple((member[:, ::-1] for member in left_in))
    out_left = run_direction(left_in, d_skip)
    out_right = run_direction(right_in, d_skip)[:, ::-1]

    def mid_local(left_part, right_part, gate_part):
        return tail_mid(left_part, right_part, gate_part, norm_gain)
    nsum, mid_pull = jax.vjp(mid_local, out_left, out_right, gate_in)
    nsum_b = nsum.astype(jnp.bfloat16)
    nsum_flat = nsum_b.reshape(batch_rows * SEQ_LEN, E)
    mixed_out = jnp.dot(nsum_flat, w_out, preferred_element_type=jnp.float32).reshape(batch_rows, SEQ_LEN, D)
    hidden32 = hidden.astype(jnp.float32)

    def head_local(mixed_in, hidden_in):
        return head_fn(mixed_in, hidden_in, final_gain, w_head)
    logits, head_pull = jax.vjp(head_local, mixed_out, hidden32)
    total_logits = logits[:SEQS] + complement(logits[SEQS:])
    vocab_hot = (tokens[..., None] == jnp.arange(VOCAB, dtype=jnp.int32)).astype(jnp.float32)
    expsum = lax.optimization_barrier(jnp.sum(jnp.exp(total_logits), axis=-1))
    cross = jnp.log(expsum) - lax.optimization_barrier(jnp.sum(total_logits * vocab_hot, axis=-1))
    mask_float = loss_mask.astype(jnp.float32)
    species_hot = (species[:, None] == jnp.arange(SPECIES, dtype=jnp.int32)[None, :]).astype(jnp.float32)
    counts = lax.optimization_barrier(jnp.sum(lax.optimization_barrier(jnp.sum(mask_float, axis=1))[:, None] * species_hot, axis=0))
    ce_sums = lax.optimization_barrier(jnp.sum(lax.optimization_barrier(jnp.sum(mask_float * cross, axis=1))[:, None] * species_hot, axis=0))
    scaled = jnp.exp(-log_var) / jnp.maximum(counts, 1.0)
    loss = jnp.sum(scaled * ce_sums + log_var).reshape(1)
    grad_log_var = 1.0 - scaled * ce_sums
    row_weight = SEQ_LEN * mask_float * lax.optimization_barrier(jnp.sum(species_hot * scaled[None, :], axis=1))[:, None]
    d_total = row_weight[..., None] * (jnp.exp(total_logits) / expsum[..., None] - vocab_hot)
    d_logits = jnp.concatenate([d_total, complement(d_total)], axis=0)
    d_mixed, d_hidden_head = head_pull(d_logits)
    d_mixed_flat = d_mixed.astype(jnp.bfloat16).reshape(batch_rows * SEQ_LEN, D)
    grad_w_out = jnp.dot(nsum_flat.T, d_mixed_flat, preferred_element_type=jnp.float32)
    d_nsum = jnp.dot(d_mixed_flat, w_out.T, preferred_element_type=jnp.float32).reshape(batch_rows, SEQ_LEN, E)
    d_left, d_right, d_gate = mid_pull(d_nsum)
    left_grads = grad_direction(left_in, d_left, d_skip)
    right_grads = tuple((member[:, ::-1] for member in grad_direction(right_in, d_right[:, ::-1], d_skip)))
    summed = tuple((left_grads[index_one] + right_grads[index_one] for index_one in range(5)))
    d_proj = prep_pull((summed[0], d_gate, summed[3], summed[4], summed[1], summed[2]))[0]
    d_proj_b = d_proj.astype(jnp.bfloat16).reshape(batch_rows * SEQ_LEN, F)
    grad_w_in = jnp.dot(hidden_flat.T, d_proj_b, preferred_element_type=jnp.float32)
    grad_hidden = jnp.dot(d_proj_b, w_in.T, preferred_element_type=jnp.float32).reshape(batch_rows, SEQ_LEN, D)
    grad_hidden = (grad_hidden + d_hidden_head).astype(jnp.bfloat16)
    return (loss, grad_log_var, grad_hidden[:SEQS], grad_hidden[SEQS:][:, ::-1], grad_w_in, grad_w_out)
```

```python
import functools

import jax
import jax.numpy as jnp
from jax import lax
from jax.experimental import pallas as pl
from jax.experimental.pallas import tpu as pltpu
from jax.sharding import PartitionSpec as P

HEADS = 16
HEAD_DIM = 64
STATE = 64
INNER = HEADS * HEAD_DIM
PAIRS = HEADS // 2
LANES = 2 * HEAD_DIM
EPSILON = 1e-05

F32 = jnp.float32
BF16 = jnp.bfloat16
HIGH = lax.Precision.HIGHEST
VMEM_BYTES = 48 * 1024 * 1024


def mm(a, b, ca=1, cb=0, precision=None):
    return lax.dot_general(
        a, b, (((ca,), (cb,)), ((), ())), precision=precision, preferred_element_type=F32
    )


def iota(shape, dim):
    return lax.broadcasted_iota(jnp.int32, shape, dim)


def pair_wide(x, j):
    first = iota((x.shape[0], LANES), 1) < HEAD_DIM
    return jnp.where(first, x[:, 2 * j : 2 * j + 1], x[:, 2 * j + 1 : 2 * j + 2])


def lanes_of(j):
    return slice(j * LANES, (j + 1) * LANES)


def softplus(x):
    return jnp.maximum(x, 0.0) + jnp.log1p(jnp.exp(-jnp.abs(x)))


def tri(length, kind):
    rows, cols = iota((length, length), 0), iota((length, length), 1)
    return jnp.where(rows >= cols if kind == "ge" else rows > cols, 1.0, 0.0).astype(F32)


def head_sum(x):
    pick = (iota((INNER, HEADS), 0) // HEAD_DIM == iota((INNER, HEADS), 1)).astype(F32).astype(BF16)
    return mm(x.astype(BF16), pick)


def steps(proj_ref, bias_ref, alog_ref):
    raw = proj_ref[0, :, 2 * INNER + 2 * STATE :].astype(F32) + bias_ref[...]
    dt = softplus(raw)
    a = -jnp.exp(alog_ref[...]) * dt
    cum = mm(tri(a.shape[0], "ge"), a, precision=HIGH)
    return raw, dt, a, cum, cum - a, cum[-1:, :]


def turned(x):
    n = x.shape[0]
    eye = jnp.where(iota((n, n), 0) == iota((n, n), 1), 1.0, 0.0).astype(F32)
    return mm(x, eye, 0, 0, HIGH)


def turned_back(x):
    n = x.shape[0]
    eye = jnp.where(iota((n, n), 0) == iota((n, n), 1), 1.0, 0.0).astype(F32)
    return mm(x, eye, 0, 0, HIGH)


def keys_of(proj_ref):
    return proj_ref[0, :, 2 * INNER : 2 * INNER + STATE]


def reads_of(proj_ref):
    return proj_ref[0, :, 2 * INNER + STATE : 2 * INNER + 2 * STATE]


def states_kernel(proj_ref, bias_ref, alog_ref, total_ref, decay_ref, wide_l, wide_r):
    unused, dt, a, cum, cex, tot = steps(proj_ref, bias_ref, alog_ref)
    w_l = jnp.exp(tot - cum) * dt
    w_r = jnp.exp(cex) * dt
    block = jnp.exp(tot)
    for j in range(PAIRS):
        s = lanes_of(j)
        v = proj_ref[0, :, s].astype(F32)
        wide_l[:, s] = (v * pair_wide(w_l, j)).astype(BF16)
        wide_r[:, s] = (v * pair_wide(w_r, j)).astype(BF16)
        decay_ref[0, :, s] = pair_wide(block, j)
    keys = keys_of(proj_ref)
    total_ref[0, 0] = mm(keys, wide_l[...], 0, 0).astype(BF16)
    total_ref[1, 0] = mm(keys, wide_r[...], 0, 0).astype(BF16)


def local_kernel(proj_ref, bias_ref, alog_ref, skip_ref, left_ref, right_ref):
    unused, dt, a, cum, cex, tot = steps(proj_ref, bias_ref, alog_ref)
    n = cum.shape[0]
    cum_t, cex_t, dt_t = turned(cum), turned(cex), turned(dt)
    score = mm(reads_of(proj_ref), keys_of(proj_ref), 1, 1)
    t, s = iota((n, n), 0), iota((n, n), 1)
    first = iota((n, LANES), 1) < HEAD_DIM
    zero = jnp.zeros((n, LANES), BF16)
    for j in range(PAIRS):
        lanes = lanes_of(j)
        v = proj_ref[0, :, lanes]
        left, right = [], []
        for h in (2 * j, 2 * j + 1):
            gap = jnp.where(
                t >= s,
                cum[:, h : h + 1] - cum_t[h : h + 1, :],
                cex_t[h : h + 1, :] - cex[:, h : h + 1],
            )
            mix = jnp.exp(jnp.minimum(gap, 0.0)) * score * dt_t[h : h + 1, :]
            left.append(jnp.where(t >= s, mix, 0.0).astype(BF16))
            right.append(jnp.where(t <= s, mix, 0.0).astype(BF16))
        stacked = jnp.concatenate([jnp.where(first, v, zero), jnp.where(first, zero, v)], axis=0)
        skip = pair_wide(skip_ref[...], j) * v.astype(F32)
        left_ref[0, :, lanes] = mm(jnp.concatenate(left, axis=1), stacked) + skip
        right_ref[0, :, lanes] = mm(jnp.concatenate(right, axis=1), stacked) + skip


def out_kernel(
    proj_ref,
    carry_ref,
    left_in,
    right_in,
    hidden_ref,
    bias_ref,
    alog_ref,
    gain_ref,
    wout_ref,
    final_ref,
    head_ref,
    left_ref,
    right_ref,
    nsum_ref,
    res_ref,
    logit_ref,
):
    unused, dt, a, cum, cex, tot = steps(proj_ref, bias_ref, alog_ref)
    e_l, e_r = jnp.exp(cum), jnp.exp(tot - cex)
    reads = reads_of(proj_ref)
    from_l = mm(reads, carry_ref[0, 0])
    from_r = mm(reads, carry_ref[1, 0])
    for j in range(PAIRS):
        s = lanes_of(j)
        left_ref[0, :, s] = left_in[0, :, s] + pair_wide(e_l, j) * from_l[:, s]
        right_ref[0, :, s] = right_in[0, :, s] + pair_wide(e_r, j) * from_r[:, s]
    gate = proj_ref[0, :, INNER : 2 * INNER].astype(F32)
    gated = gate * jax.nn.sigmoid(gate)
    u_l = left_ref[0] * gated
    u_r = right_ref[0] * gated
    k_l = lax.rsqrt(jnp.mean(u_l * u_l, axis=1, keepdims=True) + EPSILON)
    k_r = lax.rsqrt(jnp.mean(u_r * u_r, axis=1, keepdims=True) + EPSILON)
    nsum = ((u_l * k_l + u_r * k_r) * gain_ref[...]).astype(BF16)
    nsum_ref[0] = nsum
    res = hidden_ref[0].astype(F32) + mm(nsum, wout_ref[...])
    res_ref[0] = res
    normed = res * lax.rsqrt(jnp.mean(res * res, axis=1, keepdims=True) + EPSILON) * final_ref[...]
    logit_ref[0] = mm(head_ref[...], normed, 1, 1, HIGH)


def head_kernel(
    proj_ref,
    pack_ref,
    res_ref,
    left_ref,
    right_ref,
    bias_ref,
    alog_ref,
    gain_ref,
    wout_ref,
    final_ref,
    head_ref,
    ce_ref,
    dres_ref,
    dmix_ref,
    dleft_ref,
    dright_ref,
    dgate_ref,
    dstate_ref,
    wide_l,
    wide_r,
    *,
    vocab,
):
    total = pack_ref[0, :8]
    token, weight, mask = pack_ref[0, 8:9], pack_ref[0, 9:10], pack_ref[0, 10:11]
    which = iota(total.shape, 0)
    powers = jnp.where(which < vocab, jnp.exp(total), 0.0)
    expsum = jnp.sum(powers, axis=0, keepdims=True)
    hot = jnp.where(which.astype(F32) == token, 1.0, 0.0)
    ce_ref[0] = mask * (jnp.log(expsum) - jnp.sum(total * hot, axis=0, keepdims=True))
    d_logit = weight * (powers / expsum - hot)
    d_normed = mm(d_logit, head_ref[...], 0, 0, HIGH) * final_ref[...]
    res = res_ref[0]
    k = lax.rsqrt(jnp.mean(res * res, axis=1, keepdims=True) + EPSILON)
    d_res = k * (d_normed - res * (k * k * jnp.mean(d_normed * res, axis=1, keepdims=True)))
    dres_ref[0] = d_res
    d_mix = d_res.astype(BF16)
    dmix_ref[0] = d_mix
    d_sum = mm(d_mix, wout_ref[...], 1, 1) * gain_ref[...]
    gate = proj_ref[0, :, INNER : 2 * INNER].astype(F32)
    sig = jax.nn.sigmoid(gate)
    gated = gate * sig
    d_gated = jnp.zeros_like(gate)
    for source, target in ((left_ref, dleft_ref), (right_ref, dright_ref)):
        out = source[0]
        u = out * gated
        k = lax.rsqrt(jnp.mean(u * u, axis=1, keepdims=True) + EPSILON)
        d_u = k * (d_sum - u * (k * k * jnp.mean(d_sum * u, axis=1, keepdims=True)))
        target[0] = (d_u * gated).astype(BF16)
        d_gated = d_gated + d_u * out
    dgate_ref[0] = (d_gated * (sig + gated * (1.0 - sig))).astype(BF16)
    unused, dt, a, cum, cex, tot = steps(proj_ref, bias_ref, alog_ref)
    e_l, e_r = jnp.exp(cum), jnp.exp(tot - cex)
    for j in range(PAIRS):
        s = lanes_of(j)
        wide_l[:, s] = (dleft_ref[0, :, s].astype(F32) * pair_wide(e_l, j)).astype(BF16)
        wide_r[:, s] = (dright_ref[0, :, s].astype(F32) * pair_wide(e_r, j)).astype(BF16)
    reads = reads_of(proj_ref)
    dstate_ref[0, 0] = mm(reads, wide_l[...], 0, 0).astype(BF16)
    dstate_ref[1, 0] = mm(reads, wide_r[...], 0, 0).astype(BF16)


def adjoint_kernel(
    proj_ref,
    carry_ref,
    dleft_ref,
    dright_ref,
    bias_ref,
    alog_ref,
    skip_ref,
    dval_ref,
    dkey_ref,
    dread_ref,
    da_ref,
    ddt_ref,
    cols_l,
    cols_r,
    wide_l,
    wide_r,
):
    unused, dt, a, cum, cex, tot = steps(proj_ref, bias_ref, alog_ref)
    n = cum.shape[0]
    cum_t, cex_t = turned(cum), turned(cex)
    keys, reads = keys_of(proj_ref), reads_of(proj_ref)
    score = mm(keys, reads, 1, 1)
    s, t = iota((n, n), 0), iota((n, n), 1)
    first = iota((n, LANES), 1) < HEAD_DIM
    zero = jnp.zeros((n, LANES), BF16)
    d_score = jnp.zeros((n, n), F32)
    row_h = jnp.zeros((n, LANES), F32)
    row_l = jnp.zeros((n, LANES), F32)
    row_r = jnp.zeros((n, LANES), F32)
    e_l, e_r = jnp.exp(cum), jnp.exp(tot - cex)
    for j in range(PAIRS):
        lanes = lanes_of(j)
        v = proj_ref[0, :, lanes]
        d_l, d_r = dleft_ref[0, :, lanes], dright_ref[0, :, lanes]
        v_split = jnp.concatenate([jnp.where(first, v, zero), jnp.where(first, zero, v)], axis=0)
        d_mix = mm(v_split, jnp.concatenate([d_l, d_r], axis=0), 1, 1)
        mixes, sums_h, sums_l, sums_r = [], [], [], []
        for i, h in enumerate((2 * j, 2 * j + 1)):
            gap = jnp.where(
                t >= s,
                cum_t[h : h + 1, :] - cum[:, h : h + 1],
                cex[:, h : h + 1] - cex_t[h : h + 1, :],
            )
            decay = jnp.exp(jnp.minimum(gap, 0.0))
            step = dt[:, h : h + 1]
            d_l_mix = d_mix[i * n : (i + 1) * n, :n]
            d_r_mix = d_mix[i * n : (i + 1) * n, n:]
            scaled = decay * (
                jnp.where(t >= s, d_l_mix, 0.0) + jnp.where(t <= s, d_r_mix, 0.0)
            )
            with_step = scaled * step
            d_score = d_score + with_step
            flow = with_step * score
            flow_l = jnp.where(t > s, flow, 0.0)
            flow_r = jnp.where(t < s, flow, 0.0)
            cols_l[h : h + 1, :] = jnp.sum(flow_l, axis=0, keepdims=True)
            cols_r[h : h + 1, :] = jnp.sum(flow_r, axis=0, keepdims=True)
            sums_h.append((scaled * score).astype(BF16))
            sums_l.append(flow_l.astype(BF16))
            sums_r.append(flow_r.astype(BF16))
            mix = decay * score * step
            mixes.append(jnp.where(t >= s, mix, 0.0).astype(BF16))
            mixes.append(jnp.where(t <= s, mix, 0.0).astype(BF16))
        pick_rows, pick_cols = iota((2 * n, LANES), 0), iota((2 * n, LANES), 1)
        pick = (
            jnp.where(pick_cols == 2 * j + (pick_rows >= n).astype(jnp.int32), 1.0, 0.0)
            .astype(F32)
            .astype(BF16)
        )
        row_h = row_h + mm(jnp.concatenate(sums_h, axis=1), pick)
        row_l = row_l + mm(jnp.concatenate(sums_l, axis=1), pick)
        row_r = row_r + mm(jnp.concatenate(sums_r, axis=1), pick)
        d_split = jnp.concatenate(
            [
                jnp.where(first, d_l, zero),
                jnp.where(first, d_r, zero),
                jnp.where(first, zero, d_l),
                jnp.where(first, zero, d_r),
            ],
            axis=0,
        )
        both = d_l.astype(F32) + d_r.astype(F32)
        dval_ref[0, :, lanes] = (
            mm(jnp.concatenate(mixes, axis=1), d_split) + pair_wide(skip_ref[...], j) * both
        )
        wide_l[:, lanes] = (d_l.astype(F32) * pair_wide(e_l, j)).astype(BF16)
        wide_r[:, lanes] = (d_r.astype(F32) * pair_wide(e_r, j)).astype(BF16)
    carry_l, carry_r = carry_ref[0, 0], carry_ref[1, 0]
    d_score_b = d_score.astype(BF16)
    dkey_ref[0] = mm(d_score_b, reads)
    dread_ref[0] = (
        mm(d_score_b, keys, 0, 0)
        + mm(wide_l[...], carry_l, 1, 1)
        + mm(wide_r[...], carry_r, 1, 1)
    )
    d_cum = (
        head_sum(wide_l[...].astype(F32) * mm(reads, carry_l))
        + turned_back(cols_l[...])
        - row_l[:, :HEADS]
    )
    d_rcum = head_sum(wide_r[...].astype(F32) * mm(reads, carry_r))
    d_cex = row_r[:, :HEADS] - turned_back(cols_r[...])
    ge, gt = tri(n, "ge"), tri(n, "gt")
    da_ref[0] = mm(ge, d_cum, 0, 0, HIGH) + mm(gt, d_cex, 0, 0, HIGH) + mm(ge, d_rcum, 1, 0, HIGH)
    ddt_ref[0] = row_h[:, :HEADS]


def finish_kernel(
    proj_ref,
    carry_ref,
    next_ref,
    dval_in,
    dkey_in,
    dread_in,
    da_in,
    ddt_in,
    bias_ref,
    alog_ref,
    dproj_ref,
    wide_l,
    wide_r,
):
    raw, dt, a, cum, cex, tot = steps(proj_ref, bias_ref, alog_ref)
    keys = keys_of(proj_ref)
    f_l, f_r = jnp.exp(tot - cum), jnp.exp(cex)
    w_l, w_r = f_l * dt, f_r * dt
    next_l, next_r = next_ref[0, 0], next_ref[1, 0]
    z_l, z_r = mm(keys, next_l), mm(keys, next_r)
    for j in range(PAIRS):
        s = lanes_of(j)
        v = proj_ref[0, :, s].astype(F32)
        wide_w_l, wide_w_r = pair_wide(w_l, j), pair_wide(w_r, j)
        dproj_ref[0, :, s] = (
            dval_in[0, :, s] + wide_w_l * z_l[:, s] + wide_w_r * z_r[:, s]
        ).astype(BF16)
        wide_l[:, s] = (v * wide_w_l).astype(BF16)
        wide_r[:, s] = (v * wide_w_r).astype(BF16)
    values = proj_ref[0, :, :INNER].astype(F32)
    dw_l, dw_r = head_sum(values * z_l), head_sum(values * z_r)
    d_key = dkey_in[0] + mm(wide_l[...], next_l, 1, 1) + mm(wide_r[...], next_r, 1, 1)
    dproj_ref[0, :, INNER : INNER + STATE] = d_key.astype(BF16)
    dproj_ref[0, :, INNER + STATE : INNER + 2 * STATE] = dread_in[0].astype(BF16)
    through = jnp.sum(
        next_l.astype(F32) * carry_ref[0, 0].astype(F32)
        + next_r.astype(F32) * carry_ref[1, 0].astype(F32),
        axis=0,
        keepdims=True,
    )
    through = head_sum(jnp.broadcast_to(through, (8, INNER)))[:1]
    q_l, q_r = dw_l * w_l, dw_r * w_r
    n = cum.shape[0]
    ge, gt = tri(n, "ge"), tri(n, "gt")
    d_tot = jnp.exp(tot) * through + jnp.sum(q_l, axis=0, keepdims=True)
    d_a = da_in[0] + mm(gt, q_r, 0, 0, HIGH) - mm(ge, q_l, 0, 0, HIGH) + d_tot
    d_dt = ddt_in[0] + dw_l * f_l + dw_r * f_r - d_a * jnp.exp(alog_ref[...])
    dproj_ref[0, :, INNER + 2 * STATE :] = (d_dt * jax.nn.sigmoid(raw)).astype(BF16)


def by_row(shape):
    rest = (0,) * (len(shape) - 1)
    return pl.BlockSpec((1,) + tuple(shape[1:]), lambda g: (g,) + rest)


def by_dir(shape):
    rest = (0,) * (len(shape) - 2)
    return pl.BlockSpec((shape[0], 1) + tuple(shape[2:]), lambda g: (0, g) + rest)


def whole(shape):
    zeros = (0,) * len(shape)
    return pl.BlockSpec(tuple(shape), lambda g: zeros)


def call(kernel, name, operands, results, scratch=(), cost=None):
    specs = {"row": by_row, "dir": by_dir, "all": whole}
    return pl.pallas_call(
        kernel,
        name=name,
        grid=(2,),
        in_specs=[specs[kind](array.shape) for array, kind in operands],
        out_specs=[specs[kind](shape) for shape, dtype, kind in results],
        out_shape=[jax.ShapeDtypeStruct(shape, dtype) for shape, dtype, kind in results],
        scratch_shapes=[pltpu.VMEM(shape, dtype) for shape, dtype in scratch],
        compiler_params=pltpu.CompilerParams(
            dimension_semantics=("arbitrary",), vmem_limit_bytes=VMEM_BYTES
        ),
        cost_estimate=cost,
    )(*[array for array, kind in operands])


def cost(flops, moved):
    return pl.CostEstimate(flops=int(flops), transcendentals=0, bytes_accessed=int(moved))


def bits_of(axis):
    return lax.axis_size(axis).bit_length() - 1


def partner(array, axis, bit):
    return lax.ppermute(array, axis, [(i, i ^ (1 << bit)) for i in range(lax.axis_size(axis))])


def butterfly_sum(array):
    array = array + partner(array, "dp", 0) if lax.axis_size("dp") > 1 else array
    for bit in range(bits_of("ctx")):
        array = array + partner(array, "ctx", bit)
    return array


def decay_rounds(decay):
    me = lax.axis_index("ctx")
    lead_l = jnp.ones_like(decay)
    lead_r = jnp.ones_like(decay)
    rounds = []
    for bit in range(bits_of("ctx")):
        upper = ((me >> bit) & 1) == 1
        theirs = partner(decay, "ctx", bit)
        one, zero = jnp.ones_like(decay), jnp.zeros_like(decay)
        into = jnp.stack([jnp.where(upper, lead_l, zero), jnp.where(upper, zero, lead_r)])
        keep = jnp.stack([jnp.where(upper, one, theirs), jnp.where(upper, theirs, one)])
        take = jnp.stack([jnp.where(upper, decay, one), jnp.where(upper, one, decay)])
        rounds.append((upper, into, keep, take))
        lead_l = jnp.where(upper, lead_l * theirs, lead_l)
        lead_r = jnp.where(upper, lead_r, lead_r * theirs)
        decay = decay * theirs
    return rounds


def scan_blocks(total, rounds):
    entering = jnp.zeros(total.shape, F32)
    last = len(rounds) - 1
    for number, (upper, into, keep, take) in enumerate(rounds):
        if number < last:
            theirs = partner(total, "ctx", number).astype(F32)
            entering = entering + into * theirs
            total = (keep * total.astype(F32) + take * theirs).astype(BF16)
        else:
            theirs = partner(jnp.where(upper, total[1], total[0]), "ctx", number).astype(F32)
            entering = entering + into * theirs[None]
    return entering.astype(BF16)


def share_rows(mine, other_half):
    if lax.axis_size("dp") > 1:
        mine = mine + partner(other_half, "dp", 0).astype(F32)
    bits = bits_of("ctx")
    count = lax.axis_size("ctx")
    me = lax.axis_index("ctx")
    rows, cols = mine.shape
    cut = cols // 2 // 128 * 128
    parts = []
    for part, order in (
        (mine[:, :cut], list(range(bits))),
        (mine[:, cut:], list(range(1, bits)) + [0]),
    ):
        part = part.reshape((2,) * bits + (rows // count, part.shape[1]))
        left = list(range(bits - 1, -1, -1))
        for bit in order:
            at = left.index(bit)
            mine_bit = (me >> bit) & 1
            keep = lax.dynamic_index_in_dim(part, mine_bit, at, False)
            send = lax.dynamic_index_in_dim(part, 1 - mine_bit, at, False).astype(BF16)
            part = keep + partner(send, "ctx", bit).astype(F32)
            left.remove(bit)
        parts.append(part)
    return jnp.concatenate(parts, axis=1)


def weight_grad(rows_of, cotangent):
    half = rows_of.shape[1] // lax.axis_size("dp")
    me = lax.axis_index("dp")

    def part(which):
        piece = lax.dynamic_slice_in_dim(rows_of, which * half, half, 1)
        return mm(piece, cotangent, 0, 0)

    return part(me), part(1 - me).astype(BF16)


def complement(rows):
    return jnp.concatenate([rows[3::-1], rows[4:]], axis=0)


def on_device(
    h_fwd,
    h_rc,
    tokens,
    loss_mask,
    species,
    w_in,
    a_log,
    dt_bias,
    d_skip,
    norm_gain,
    w_out,
    final_gain,
    w_head,
    log_var,
):
    length, width = h_fwd.shape[1], h_fwd.shape[2]
    vocab = w_head.shape[0]
    ctx = lax.axis_size("ctx")
    rows = 2
    flat = rows * length

    hidden = jnp.concatenate([h_fwd, h_rc], axis=0)
    hidden_flat = hidden.reshape(flat, width)
    proj = mm(hidden_flat, w_in).astype(BF16).reshape(rows, length, -1)

    bias, alog, skip = dt_bias[None], a_log[None], d_skip[None]
    gain, final = norm_gain[None], final_gain[None]
    head = jnp.concatenate([w_head, jnp.zeros((8 - vocab, width), F32)], axis=0)

    mask_row = loss_mask.astype(F32)
    species_hot = (
        species[:, None] == jnp.arange(log_var.shape[0], dtype=jnp.int32)[None, :]
    ).astype(F32)
    counts = butterfly_sum(jnp.sum(mask_row, axis=1, keepdims=True) * species_hot)[0]
    scaled = jnp.exp(-log_var) / jnp.maximum(counts, 1.0)

    state_shape = (2, rows, STATE, INNER)
    wide = ((length, INNER), BF16)
    full = (rows, length, INNER)
    total, decay = call(
        states_kernel,
        "states",
        [(proj, "row"), (bias, "all"), (alog, "all")],
        [(state_shape, BF16, "dir"), ((rows, 1, INNER), F32, "row")],
        [wide, wide],
        cost(1e9, 3e6),
    )
    rounds = decay_rounds(decay)
    left_own, right_own = call(
        local_kernel,
        "local",
        [(proj, "row"), (bias, "all"), (alog, "all"), (skip, "all")],
        [(full, F32, "row"), (full, F32, "row")],
        (),
        cost(4e9, 4e6),
    )
    carry = scan_blocks(total, rounds)
    out_left, out_right, nsum, res, logits = call(
        out_kernel,
        "out",
        [
            (proj, "row"),
            (carry, "dir"),
            (left_own, "row"),
            (right_own, "row"),
            (hidden, "row"),
            (bias, "all"),
            (alog, "all"),
            (gain, "all"),
            (w_out, "all"),
            (final, "all"),
            (head, "all"),
        ],
        [
            (full, F32, "row"),
            (full, F32, "row"),
            (full, BF16, "row"),
            ((rows, length, width), F32, "row"),
            ((rows, 8, length), F32, "row"),
        ],
        (),
        cost(2e9, 8e6),
    )

    token_row = tokens.astype(F32)
    sent = jnp.concatenate([logits[0, :vocab], logits[1, :vocab], token_row, mask_row], axis=0)
    got = lax.ppermute(sent, "ctx", [(i, ctx - 1 - i) for i in range(ctx)])[:, ::-1]
    their_token = got[2 * vocab : 2 * vocab + 1]
    weight = float(length * ctx) * jnp.sum(species_hot[0] * scaled)
    unused_rows = jnp.zeros((8 - vocab, length), F32)
    their_mask = got[2 * vocab + 1 :]
    pack = jnp.stack(
        [
            jnp.concatenate(
                [
                    logits[0, :vocab] + complement(got[vocab : 2 * vocab]),
                    unused_rows,
                    token_row,
                    weight * mask_row,
                    mask_row,
                ]
            ),
            jnp.concatenate(
                [
                    logits[1, :vocab] + complement(got[:vocab]),
                    unused_rows,
                    jnp.where(their_token < 4.0, 3.0 - their_token, their_token),
                    weight * their_mask,
                    their_mask,
                ]
            ),
        ]
    )
    ce, d_res, d_mix, d_left, d_right, d_gate, d_state = call(
        functools.partial(head_kernel, vocab=vocab),
        "head",
        [
            (proj, "row"),
            (pack, "row"),
            (res, "row"),
            (out_left, "row"),
            (out_right, "row"),
            (bias, "all"),
            (alog, "all"),
            (gain, "all"),
            (w_out, "all"),
            (final, "all"),
            (head, "all"),
        ],
        [
            ((rows, 1, length), F32, "row"),
            ((rows, length, width), F32, "row"),
            ((rows, length, width), BF16, "row"),
            (full, BF16, "row"),
            (full, BF16, "row"),
            (full, BF16, "row"),
            (state_shape, BF16, "dir"),
        ],
        [wide, wide],
        cost(2e9, 8e6),
    )
    ce_sums = butterfly_sum(jnp.sum(ce[0], axis=1, keepdims=True) * species_hot)[0]
    d_mix_flat = d_mix.reshape(flat, width)
    d_gate_flat = d_gate.reshape(flat, INNER)
    following = scan_blocks(d_state[::-1], rounds)[::-1]
    d_val, d_key, d_read, d_a, d_dt = call(
        adjoint_kernel,
        "adjoint",
        [
            (proj, "row"),
            (carry, "dir"),
            (d_left, "row"),
            (d_right, "row"),
            (bias, "all"),
            (alog, "all"),
            (skip, "all"),
        ],
        [
            (full, F32, "row"),
            ((rows, length, STATE), F32, "row"),
            ((rows, length, STATE), F32, "row"),
            ((rows, length, HEADS), F32, "row"),
            ((rows, length, HEADS), F32, "row"),
        ],
        [((HEADS, length), F32), ((HEADS, length), F32), wide, wide],
        cost(8e9, 6e6),
    )
    early = [weight_grad(nsum.reshape(flat, INNER), d_mix_flat), weight_grad(hidden_flat, d_gate_flat)]
    early = share_rows(
        jnp.concatenate([early[0][0], early[1][0]], axis=1),
        jnp.concatenate([early[0][1], early[1][1]], axis=1),
    )
    grad_hidden = mm(d_gate_flat, w_in[:, INNER : 2 * INNER], 1, 1) + d_res.reshape(flat, width)
    (d_rest,) = call(
        finish_kernel,
        "finish",
        [
            (proj, "row"),
            (carry, "dir"),
            (following, "dir"),
            (d_val, "row"),
            (d_key, "row"),
            (d_read, "row"),
            (d_a, "row"),
            (d_dt, "row"),
            (bias, "all"),
            (alog, "all"),
        ],
        [((rows, length, INNER + 2 * STATE + HEADS), BF16, "row")],
        [wide, wide],
        cost(2e9, 5e6),
    )
    d_rest = d_rest.reshape(flat, -1)
    late = share_rows(*weight_grad(hidden_flat, d_rest))
    grad_hidden = (
        grad_hidden
        + mm(d_rest[:, :INNER], w_in[:, :INNER], 1, 1)
        + mm(d_rest[:, INNER:], w_in[:, 2 * INNER :], 1, 1)
    ).astype(BF16)
    grad_hidden = grad_hidden.reshape(rows, length, width)
    grad_w_in = jnp.concatenate([late[:, :INNER], early[:, width:], late[:, INNER:]], axis=1)
    grad_w_out = early[:, :width]
    loss = jnp.sum(scaled * ce_sums + log_var).reshape(1)
    grad_log_var = 1.0 - scaled * ce_sums
    return (loss, grad_log_var, grad_hidden[:1], grad_hidden[1:], grad_w_in, grad_w_out)


def solution(mesh):
    return jax.shard_map(
        on_device,
        mesh=mesh,
        in_specs=(
            P(("groups", "dp"), "ctx", None),
            P(("groups", "dp"), "ctx", None),
            P(("groups", "dp"), "ctx"),
            P(("groups", "dp"), "ctx"),
            P(("groups", "dp")),
            P(),
            P(),
            P(),
            P(),
            P(),
            P(),
            P(),
            P(),
            P(),
        ),
        out_specs=(
            P("groups"),
            P("groups"),
            P(("groups", "dp"), "ctx", None),
            P(("groups", "dp"), "ctx", None),
            P(("groups", "dp", "ctx"), None),
            P(("groups", "dp", "ctx"), None),
        ),
        check_vma=False,
    )
```

```python
import functools

import jax
import jax.numpy as jnp
from jax import lax
from jax.experimental import pallas as pl
from jax.experimental.pallas import tpu as pltpu
from jax.sharding import PartitionSpec as P

HEADS = 16
HEAD_DIM = 64
STATE = 64
INNER = HEADS * HEAD_DIM
PAIRS = HEADS // 2
LANES = 2 * HEAD_DIM
EPSILON = 1e-05

F32 = jnp.float32
BF16 = jnp.bfloat16
HIGH = lax.Precision.HIGHEST
VMEM_BYTES = 24 * 1024 * 1024


def mm(a, b, ca=1, cb=0, precision=None):
    return lax.dot_general(
        a, b, (((ca,), (cb,)), ((), ())), precision=precision, preferred_element_type=F32
    )


def iota(shape, dim):
    return lax.broadcasted_iota(jnp.int32, shape, dim)


def pair_wide(x, j):
    first = iota((x.shape[0], LANES), 1) < HEAD_DIM
    return jnp.where(first, x[:, 2 * j : 2 * j + 1], x[:, 2 * j + 1 : 2 * j + 2])


def lanes_of(j):
    return slice(j * LANES, (j + 1) * LANES)


def softplus(x):
    return jnp.maximum(x, 0.0) + jnp.log1p(jnp.exp(-jnp.abs(x)))


def tri(length, kind):
    rows, cols = iota((length, length), 0), iota((length, length), 1)
    return jnp.where(rows >= cols if kind == "ge" else rows > cols, 1.0, 0.0).astype(F32)


def head_sum(x):
    pick = (iota((INNER, HEADS), 0) // HEAD_DIM == iota((INNER, HEADS), 1)).astype(F32).astype(BF16)
    return mm(x.astype(BF16), pick)


def steps(proj_ref, bias_ref, alog_ref):
    raw = proj_ref[0, :, 2 * INNER + 2 * STATE :].astype(F32) + bias_ref[...]
    dt = softplus(raw)
    a = -jnp.exp(alog_ref[...]) * dt
    cum = mm(tri(a.shape[0], "ge"), a, precision=HIGH)
    return raw, dt, a, cum, cum - a, cum[-1:, :]


def turned(x):
    n = x.shape[0]
    eye = jnp.where(iota((n, n), 0) == iota((n, n), 1), 1.0, 0.0).astype(F32)
    return mm(x, eye, 0, 0, HIGH)


def turned_back(x):
    n = x.shape[0]
    eye = jnp.where(iota((n, n), 0) == iota((n, n), 1), 1.0, 0.0).astype(F32)
    return mm(x, eye, 0, 0, HIGH)


def keys_of(proj_ref):
    return proj_ref[0, :, 2 * INNER : 2 * INNER + STATE]


def reads_of(proj_ref):
    return proj_ref[0, :, 2 * INNER + STATE : 2 * INNER + 2 * STATE]


def front_kernel(
    fwd_ref,
    rc_ref,
    win_ref,
    bias_ref,
    alog_ref,
    mask_ref,
    species_ref,
    proj_ref,
    total_ref,
    small_ref,
    wide_l,
    wide_r,
):
    row = pl.program_id(0)
    hidden = jnp.where(row == 0, fwd_ref[0], rc_ref[0])
    proj_ref[0] = mm(hidden, win_ref[...], 1, 1).astype(BF16)
    unused, dt, a, cum, cex, tot = steps(proj_ref, bias_ref, alog_ref)
    w_l = jnp.exp(tot - cum) * dt
    w_r = jnp.exp(cex) * dt
    block = jnp.exp(tot)
    for j in range(PAIRS):
        s = lanes_of(j)
        v = proj_ref[0, :, s].astype(F32)
        wide_l[:, s] = (v * pair_wide(w_l, j)).astype(BF16)
        wide_r[:, s] = (v * pair_wide(w_r, j)).astype(BF16)
        small_ref[pl.ds(row, 1), :, s] = pair_wide(block, j)[None]
    keys = keys_of(proj_ref)
    total_ref[0, 0] = mm(keys, wide_l[...], 0, 0).astype(BF16)
    total_ref[0, 1] = mm(keys, wide_r[...], 0, 0).astype(BF16)

    @pl.when(row == 0)
    def _():
        scored = jnp.sum(mask_ref[...].astype(F32), axis=1, keepdims=True)
        small_ref[2] = jnp.where(iota((1, INNER), 1) == species_ref[...], scored, 0.0)


def local_kernel(proj_ref, bias_ref, alog_ref, skip_ref, left_ref, right_ref):
    unused, dt, a, cum, cex, tot = steps(proj_ref, bias_ref, alog_ref)
    n = cum.shape[0]
    cum_t, cex_t, dt_t = turned(cum), turned(cex), turned(dt)
    score = mm(reads_of(proj_ref), keys_of(proj_ref), 1, 1)
    t, s = iota((n, n), 0), iota((n, n), 1)
    first = iota((n, LANES), 1) < HEAD_DIM
    zero = jnp.zeros((n, LANES), BF16)
    for j in range(PAIRS):
        lanes = lanes_of(j)
        v = proj_ref[0, :, lanes]
        left, right = [], []
        for h in (2 * j, 2 * j + 1):
            gap = jnp.where(
                t >= s,
                cum[:, h : h + 1] - cum_t[h : h + 1, :],
                cex_t[h : h + 1, :] - cex[:, h : h + 1],
            )
            mix = jnp.exp(jnp.minimum(gap, 0.0)) * score * dt_t[h : h + 1, :]
            left.append(jnp.where(t >= s, mix, 0.0).astype(BF16))
            right.append(jnp.where(t <= s, mix, 0.0).astype(BF16))
        stacked = jnp.concatenate([jnp.where(first, v, zero), jnp.where(first, zero, v)], axis=0)
        skip = pair_wide(skip_ref[...], j) * v.astype(F32)
        left_ref[0, :, lanes] = mm(jnp.concatenate(left, axis=1), stacked) + skip
        right_ref[0, :, lanes] = mm(jnp.concatenate(right, axis=1), stacked) + skip


def out_kernel(
    proj_ref,
    carry_ref,
    left_in,
    right_in,
    fwd_ref,
    rc_ref,
    bias_ref,
    alog_ref,
    gain_ref,
    wout_ref,
    final_ref,
    head_ref,
    token_ref,
    mask_ref,
    left_ref,
    right_ref,
    nsum_ref,
    res_ref,
    sent_ref,
):
    row = pl.program_id(0)
    unused, dt, a, cum, cex, tot = steps(proj_ref, bias_ref, alog_ref)
    e_l, e_r = jnp.exp(cum), jnp.exp(tot - cex)
    reads = reads_of(proj_ref)
    from_l = mm(reads, carry_ref[0, 0])
    from_r = mm(reads, carry_ref[0, 1])
    for j in range(PAIRS):
        s = lanes_of(j)
        left_ref[0, :, s] = left_in[0, :, s] + pair_wide(e_l, j) * from_l[:, s]
        right_ref[0, :, s] = right_in[0, :, s] + pair_wide(e_r, j) * from_r[:, s]
    gate = proj_ref[0, :, INNER : 2 * INNER].astype(F32)
    gated = gate * jax.nn.sigmoid(gate)
    u_l = left_ref[0] * gated
    u_r = right_ref[0] * gated
    k_l = lax.rsqrt(jnp.mean(u_l * u_l, axis=1, keepdims=True) + EPSILON)
    k_r = lax.rsqrt(jnp.mean(u_r * u_r, axis=1, keepdims=True) + EPSILON)
    nsum = ((u_l * k_l + u_r * k_r) * gain_ref[...]).astype(BF16)
    nsum_ref[...] = nsum
    hidden = jnp.where(row == 0, fwd_ref[0], rc_ref[0])
    res = hidden.astype(F32) + mm(nsum, wout_ref[...])
    res_ref[0] = res
    normed = res * lax.rsqrt(jnp.mean(res * res, axis=1, keepdims=True) + EPSILON) * final_ref[...]
    sent_ref[pl.ds(row * 8, 8), :] = mm(head_ref[...], normed, 1, 1, HIGH)

    @pl.when(row == 0)
    def _():
        line = iota((8, normed.shape[0]), 0)
        sent_ref[16:24, :] = jnp.where(
            line == 0,
            token_ref[...].astype(F32),
            jnp.where(line == 1, mask_ref[...].astype(F32), 0.0),
        )


def head_kernel(
    proj_ref,
    sent_ref,
    got_ref,
    counts_ref,
    species_ref,
    logvar_ref,
    res_ref,
    left_ref,
    right_ref,
    bias_ref,
    alog_ref,
    gain_ref,
    wout_ref,
    final_ref,
    head_ref,
    ce_ref,
    dres_ref,
    dmix_ref,
    dleft_ref,
    dright_ref,
    dgate_ref,
    dstate_ref,
    wide_l,
    wide_r,
    *,
    vocab,
    loss_scale,
):
    row = pl.program_id(0)
    n = sent_ref.shape[1]
    mirror = jnp.where(iota((n, n), 0) + iota((n, n), 1) == n - 1, 1.0, 0.0).astype(F32)
    to, of = iota((8, 8), 0), iota((8, 8), 1)
    swap = jnp.where(jnp.where(to < 4, 3 - to, to) == of, 1.0, 0.0).astype(F32)
    other = mm(got_ref[pl.ds((1 - row) * 8, 8), :], mirror, precision=HIGH)
    total = sent_ref[pl.ds(row * 8, 8), :] + mm(swap, other, precision=HIGH)
    seen = mm(got_ref[16:24, :], mirror, precision=HIGH)
    their_token = jnp.where(seen[0:1] < 4.0, 3.0 - seen[0:1], seen[0:1])
    token = jnp.where(row == 0, sent_ref[16:17, :], their_token)
    mask = jnp.where(row == 0, sent_ref[17:18, :], seen[1:2])
    kinds = logvar_ref.shape[1]
    scaled = jnp.exp(-logvar_ref[...]) / jnp.maximum(counts_ref[0, :, :kinds], 1.0)
    chosen = iota((1, kinds), 1) == species_ref[...]
    weight = loss_scale * mask * jnp.sum(jnp.where(chosen, scaled, 0.0), axis=1, keepdims=True)
    which = iota(total.shape, 0)
    powers = jnp.where(which < vocab, jnp.exp(total), 0.0)
    expsum = jnp.sum(powers, axis=0, keepdims=True)
    hot = jnp.where(which.astype(F32) == token, 1.0, 0.0)

    @pl.when(row == 0)
    def _():
        ce = mask * (jnp.log(expsum) - jnp.sum(total * hot, axis=0, keepdims=True))
        ce = jnp.sum(ce, axis=1, keepdims=True)
        ce_ref[...] = jnp.where(iota((1, n), 1) == species_ref[...], ce, 0.0)

    d_logit = weight * (powers / expsum - hot)
    d_normed = mm(d_logit, head_ref[...], 0, 0, HIGH) * final_ref[...]
    res = res_ref[0]
    k = lax.rsqrt(jnp.mean(res * res, axis=1, keepdims=True) + EPSILON)
    d_res = k * (d_normed - res * (k * k * jnp.mean(d_normed * res, axis=1, keepdims=True)))
    dres_ref[0] = d_res
    d_mix = d_res.astype(BF16)
    dmix_ref[...] = d_mix
    d_sum = mm(d_mix, wout_ref[...], 1, 1) * gain_ref[...]
    gate = proj_ref[0, :, INNER : 2 * INNER].astype(F32)
    sig = jax.nn.sigmoid(gate)
    gated = gate * sig
    d_gated = jnp.zeros_like(gate)
    for source, target in ((left_ref, dleft_ref), (right_ref, dright_ref)):
        out = source[0]
        u = out * gated
        k = lax.rsqrt(jnp.mean(u * u, axis=1, keepdims=True) + EPSILON)
        d_u = k * (d_sum - u * (k * k * jnp.mean(d_sum * u, axis=1, keepdims=True)))
        target[0] = (d_u * gated).astype(BF16)
        d_gated = d_gated + d_u * out
    dgate_ref[...] = (d_gated * (sig + gated * (1.0 - sig))).astype(BF16)
    unused, dt, a, cum, cex, tot = steps(proj_ref, bias_ref, alog_ref)
    e_l, e_r = jnp.exp(cum), jnp.exp(tot - cex)
    for j in range(PAIRS):
        s = lanes_of(j)
        wide_l[:, s] = (dleft_ref[0, :, s].astype(F32) * pair_wide(e_l, j)).astype(BF16)
        wide_r[:, s] = (dright_ref[0, :, s].astype(F32) * pair_wide(e_r, j)).astype(BF16)
    reads = reads_of(proj_ref)
    dstate_ref[0, 1] = mm(reads, wide_l[...], 0, 0).astype(BF16)
    dstate_ref[0, 0] = mm(reads, wide_r[...], 0, 0).astype(BF16)


def adjoint_kernel(
    proj_ref,
    carry_ref,
    dleft_ref,
    dright_ref,
    bias_ref,
    alog_ref,
    skip_ref,
    dval_ref,
    dkey_ref,
    dread_ref,
    da_ref,
    ddt_ref,
    cols_l,
    cols_r,
    wide_l,
    wide_r,
):
    unused, dt, a, cum, cex, tot = steps(proj_ref, bias_ref, alog_ref)
    n = cum.shape[0]
    cum_t, cex_t = turned(cum), turned(cex)
    keys, reads = keys_of(proj_ref), reads_of(proj_ref)
    score = mm(keys, reads, 1, 1)
    s, t = iota((n, n), 0), iota((n, n), 1)
    first = iota((n, LANES), 1) < HEAD_DIM
    zero = jnp.zeros((n, LANES), BF16)
    d_score = jnp.zeros((n, n), F32)
    row_h = jnp.zeros((n, LANES), F32)
    row_l = jnp.zeros((n, LANES), F32)
    row_r = jnp.zeros((n, LANES), F32)
    e_l, e_r = jnp.exp(cum), jnp.exp(tot - cex)
    for j in range(PAIRS):
        lanes = lanes_of(j)
        v = proj_ref[0, :, lanes]
        d_l, d_r = dleft_ref[0, :, lanes], dright_ref[0, :, lanes]
        v_split = jnp.concatenate([jnp.where(first, v, zero), jnp.where(first, zero, v)], axis=0)
        d_mix = mm(v_split, jnp.concatenate([d_l, d_r], axis=0), 1, 1)
        mixes, sums_h, sums_l, sums_r = [], [], [], []
        for i, h in enumerate((2 * j, 2 * j + 1)):
            gap = jnp.where(
                t >= s,
                cum_t[h : h + 1, :] - cum[:, h : h + 1],
                cex[:, h : h + 1] - cex_t[h : h + 1, :],
            )
            decay = jnp.exp(jnp.minimum(gap, 0.0))
            step = dt[:, h : h + 1]
            d_l_mix = d_mix[i * n : (i + 1) * n, :n]
            d_r_mix = d_mix[i * n : (i + 1) * n, n:]
            scaled = decay * (
                jnp.where(t >= s, d_l_mix, 0.0) + jnp.where(t <= s, d_r_mix, 0.0)
            )
            with_step = scaled * step
            d_score = d_score + with_step
            flow = with_step * score
            flow_l = jnp.where(t > s, flow, 0.0)
            flow_r = jnp.where(t < s, flow, 0.0)
            cols_l[h : h + 1, :] = jnp.sum(flow_l, axis=0, keepdims=True)
            cols_r[h : h + 1, :] = jnp.sum(flow_r, axis=0, keepdims=True)
            sums_h.append((scaled * score).astype(BF16))
            sums_l.append(flow_l.astype(BF16))
            sums_r.append(flow_r.astype(BF16))
            mix = decay * score * step
            mixes.append(jnp.where(t >= s, mix, 0.0).astype(BF16))
            mixes.append(jnp.where(t <= s, mix, 0.0).astype(BF16))
        pick_rows, pick_cols = iota((2 * n, LANES), 0), iota((2 * n, LANES), 1)
        pick = (
            jnp.where(pick_cols == 2 * j + (pick_rows >= n).astype(jnp.int32), 1.0, 0.0)
            .astype(F32)
            .astype(BF16)
        )
        row_h = row_h + mm(jnp.concatenate(sums_h, axis=1), pick)
        row_l = row_l + mm(jnp.concatenate(sums_l, axis=1), pick)
        row_r = row_r + mm(jnp.concatenate(sums_r, axis=1), pick)
        d_split = jnp.concatenate(
            [
                jnp.where(first, d_l, zero),
                jnp.where(first, d_r, zero),
                jnp.where(first, zero, d_l),
                jnp.where(first, zero, d_r),
            ],
            axis=0,
        )
        both = d_l.astype(F32) + d_r.astype(F32)
        dval_ref[0, :, lanes] = (
            mm(jnp.concatenate(mixes, axis=1), d_split) + pair_wide(skip_ref[...], j) * both
        )
        wide_l[:, lanes] = (d_l.astype(F32) * pair_wide(e_l, j)).astype(BF16)
        wide_r[:, lanes] = (d_r.astype(F32) * pair_wide(e_r, j)).astype(BF16)
    carry_l, carry_r = carry_ref[0, 0], carry_ref[0, 1]
    d_score_b = d_score.astype(BF16)
    dkey_ref[0] = mm(d_score_b, reads)
    dread_ref[0] = (
        mm(d_score_b, keys, 0, 0)
        + mm(wide_l[...], carry_l, 1, 1)
        + mm(wide_r[...], carry_r, 1, 1)
    )
    d_cum = (
        head_sum(wide_l[...].astype(F32) * mm(reads, carry_l))
        + turned_back(cols_l[...])
        - row_l[:, :HEADS]
    )
    d_rcum = head_sum(wide_r[...].astype(F32) * mm(reads, carry_r))
    d_cex = row_r[:, :HEADS] - turned_back(cols_r[...])
    ge, gt = tri(n, "ge"), tri(n, "gt")
    da_ref[0] = mm(ge, d_cum, 0, 0, HIGH) + mm(gt, d_cex, 0, 0, HIGH) + mm(ge, d_rcum, 1, 0, HIGH)
    ddt_ref[0] = row_h[:, :HEADS]


def finish_kernel(
    proj_ref,
    carry_ref,
    next_ref,
    dval_in,
    dkey_in,
    dread_in,
    da_in,
    ddt_in,
    bias_ref,
    alog_ref,
    dproj_ref,
    wide_l,
    wide_r,
):
    raw, dt, a, cum, cex, tot = steps(proj_ref, bias_ref, alog_ref)
    keys = keys_of(proj_ref)
    f_l, f_r = jnp.exp(tot - cum), jnp.exp(cex)
    w_l, w_r = f_l * dt, f_r * dt
    next_r, next_l = next_ref[0, 0], next_ref[0, 1]
    z_l, z_r = mm(keys, next_l), mm(keys, next_r)
    for j in range(PAIRS):
        s = lanes_of(j)
        v = proj_ref[0, :, s].astype(F32)
        wide_w_l, wide_w_r = pair_wide(w_l, j), pair_wide(w_r, j)
        dproj_ref[:, s] = (
            dval_in[0, :, s] + wide_w_l * z_l[:, s] + wide_w_r * z_r[:, s]
        ).astype(BF16)
        wide_l[:, s] = (v * wide_w_l).astype(BF16)
        wide_r[:, s] = (v * wide_w_r).astype(BF16)
    values = proj_ref[0, :, :INNER].astype(F32)
    dw_l, dw_r = head_sum(values * z_l), head_sum(values * z_r)
    d_key = dkey_in[0] + mm(wide_l[...], next_l, 1, 1) + mm(wide_r[...], next_r, 1, 1)
    dproj_ref[:, INNER : INNER + STATE] = d_key.astype(BF16)
    dproj_ref[:, INNER + STATE : INNER + 2 * STATE] = dread_in[0].astype(BF16)
    through = jnp.sum(
        next_l.astype(F32) * carry_ref[0, 0].astype(F32)
        + next_r.astype(F32) * carry_ref[0, 1].astype(F32),
        axis=0,
        keepdims=True,
    )
    through = head_sum(jnp.broadcast_to(through, (8, INNER)))[:1]
    q_l, q_r = dw_l * w_l, dw_r * w_r
    n = cum.shape[0]
    ge, gt = tri(n, "ge"), tri(n, "gt")
    d_tot = jnp.exp(tot) * through + jnp.sum(q_l, axis=0, keepdims=True)
    d_a = da_in[0] + mm(gt, q_r, 0, 0, HIGH) - mm(ge, q_l, 0, 0, HIGH) + d_tot
    d_dt = ddt_in[0] + dw_l * f_l + dw_r * f_r - d_a * jnp.exp(alog_ref[...])
    dproj_ref[:, INNER + 2 * STATE :] = (d_dt * jax.nn.sigmoid(raw)).astype(BF16)


def input_kernel(rest_ref, gate_ref, win_ref, dres_ref, fwd_ref, rc_ref):
    row = pl.program_id(0)
    grad = (
        dres_ref[0]
        + mm(gate_ref[...], win_ref[INNER : 2 * INNER])
        + mm(rest_ref[:, :INNER], win_ref[:INNER])
        + mm(rest_ref[:, INNER:], win_ref[2 * INNER :])
    ).astype(BF16)

    @pl.when(row == 0)
    def _():
        fwd_ref[0] = grad

    @pl.when(row == 1)
    def _():
        rc_ref[0] = grad


def weight_kernel(
    place_ref, rows_ref, their_rows_ref, cot_ref, their_cot_ref, send_ref, keep_ref, both, *, block
):
    half = their_rows_ref.shape[1]
    mine = jnp.where(place_ref[0] == 0, rows_ref[:, :half], rows_ref[:, half:])
    both[...] = mm(mine, cot_ref[...], 0, 0) + mm(their_rows_ref[...], their_cot_ref[...], 0, 0)
    side = place_ref[1]
    for i in range(keep_ref.shape[0] // block):
        here = slice(i * block, (i + 1) * block)
        keep_ref[here, :] = both[pl.ds((2 * i + side) * block, block), :]
        send_ref[here, :] = both[pl.ds((2 * i + 1 - side) * block, block), :].astype(BF16)


def by_row(shape):
    rest = (0,) * (len(shape) - 1)
    return pl.BlockSpec((1,) + tuple(shape[1:]), lambda g: (g,) + rest)


def by_half(shape):
    return pl.BlockSpec((shape[0] // 2, shape[1]), lambda g: (g, 0))


def whole(shape):
    zeros = (0,) * len(shape)
    return pl.BlockSpec(tuple(shape), lambda g: zeros)


FAR = ("row hbm", "half hbm", "all hbm")


def far(array):
    return pltpu.with_memory_space_constraint(array, pltpu.HBM)


def placed(shape, dtype, kind):
    return pltpu.HBM(shape, dtype) if kind in FAR else jax.ShapeDtypeStruct(shape, dtype)


def call(kernel, name, operands, results, scratch=(), cost=None):
    specs = {"row": by_row, "half": by_half, "all": whole}
    specs.update({kind + " hbm": spec for kind, spec in list(specs.items())})
    return pl.pallas_call(
        kernel,
        name=name,
        grid=(2,),
        in_specs=[specs[kind](array.shape) for array, kind in operands],
        out_specs=[specs[kind](shape) for shape, dtype, kind in results],
        out_shape=[placed(shape, dtype, kind) for shape, dtype, kind in results],
        scratch_shapes=[pltpu.VMEM(shape, dtype) for shape, dtype in scratch],
        compiler_params=pltpu.CompilerParams(
            dimension_semantics=("arbitrary",), vmem_limit_bytes=VMEM_BYTES
        ),
        cost_estimate=cost,
    )(*[far(array) if kind in FAR else array for array, kind in operands])


def cost(flops, moved):
    return pl.CostEstimate(flops=int(flops), transcendentals=0, bytes_accessed=int(moved))


def bits_of(axis):
    return lax.axis_size(axis).bit_length() - 1


def partner(array, axis, bit):
    return lax.ppermute(array, axis, [(i, i ^ (1 << bit)) for i in range(lax.axis_size(axis))])


def together(*arrays):
    return lax.optimization_barrier(arrays)


class Sum:
    def __init__(self, array):
        self.array = array
        self.left = [("ctx", bit) for bit in range(bits_of("ctx"))]
        self.left += [("dp", bit) for bit in range(bits_of("dp"))]

    def step(self):
        if self.left:
            axis, bit = self.left.pop(0)
            self.array = self.array + partner(self.array, axis, bit)

    def finish(self):
        while self.left:
            self.step()
        return self.array


def is_upper(bit):
    return ((lax.axis_index("ctx") >> bit) & 1) == 1


def factors(upper, lead_l, lead_r, decay, theirs):
    one, zero = jnp.ones_like(decay), jnp.zeros_like(decay)
    into = jnp.stack([jnp.where(upper, lead_l, zero), jnp.where(upper, zero, lead_r)], axis=1)
    keep = jnp.stack([jnp.where(upper, one, theirs), jnp.where(upper, theirs, one)], axis=1)
    take = jnp.stack([jnp.where(upper, decay, one), jnp.where(upper, one, decay)], axis=1)
    return into, keep, take


def scan_round(total, entering, bit, last, into_keep_take, theirs):
    into, keep, take = into_keep_take
    theirs = theirs.astype(F32)
    if last:
        return None, entering + into * theirs[:, None]
    return (
        (keep * total.astype(F32) + take * theirs).astype(BF16),
        entering + into * theirs,
    )


def to_send(total, bit, last):
    return jnp.where(is_upper(bit), total[:, 1], total[:, 0]) if last else total


def scan_states(total, small):
    bits = bits_of("ctx")
    entering = jnp.zeros(total.shape, F32)
    rows = total.shape[0]
    lead_l = jnp.ones((rows, 1, INNER), F32)
    lead_r = lead_l
    rounds = []
    for bit in range(bits):
        last, upper = bit == bits - 1, is_upper(bit)
        sent, small = together(to_send(total, bit, last), small)
        theirs = partner(sent, "ctx", bit)
        theirs_small = partner(small, "ctx", bit)
        decay, their_decay = small[:rows], theirs_small[:rows]
        rounds.append(factors(upper, lead_l, lead_r, decay, their_decay))
        total, entering = scan_round(total, entering, bit, last, rounds[-1], theirs)
        lead_l = jnp.where(upper, lead_l * their_decay, lead_l)
        lead_r = jnp.where(upper, lead_r, lead_r * their_decay)
        small = jnp.concatenate([decay * their_decay, small[rows:] + theirs_small[rows:]], axis=0)
    return entering.astype(BF16), rounds, small[rows:]


def over_cores(array):
    return lax.ppermute(array, "dp", [(0, 1), (1, 0)])


def their_half(rows_of):
    half = rows_of.shape[1] // 2
    return over_cores(
        jnp.where(lax.axis_index("dp") == 0, rows_of[:, half:], rows_of[:, :half])
    )


class RowShare:
    def __init__(self, rows_of, theirs, cotangent):
        ctx = lax.axis_size("ctx")
        their_cot = over_cores(cotangent)
        place = jnp.stack([lax.axis_index("dp"), lax.axis_index("ctx") & 1]).astype(jnp.int32)
        half, cols = rows_of.shape[1] // 2, cotangent.shape[1]
        block = half // ctx
        vmem = pl.BlockSpec(memory_space=pltpu.VMEM)
        self.send, self.mine = pl.pallas_call(
            functools.partial(weight_kernel, block=block),
            name="weight",
            in_specs=[pl.BlockSpec(memory_space=pltpu.SMEM), vmem, vmem, vmem, vmem],
            out_specs=[vmem, vmem],
            out_shape=[
                jax.ShapeDtypeStruct((half // 2, cols), BF16),
                jax.ShapeDtypeStruct((half // 2, cols), F32),
            ],
            scratch_shapes=[pltpu.VMEM((half, cols), F32)],
            compiler_params=pltpu.CompilerParams(vmem_limit_bytes=VMEM_BYTES),
            cost_estimate=cost(1.2e9, 6e6),
        )(place, rows_of, theirs, cotangent, their_cot)
        self.bit = 0
        self.bits = bits_of("ctx")
        self.block = block

    def done(self):
        return self.bit == self.bits

    def pass_on(self, got):
        self.mine = self.mine + got.astype(F32)
        self.bit += 1
        if not self.done():
            cols = self.mine.shape[1]
            pairs = self.mine.reshape(-1, 2, self.block, cols)
            side = (lax.axis_index("ctx") >> self.bit) & 1
            self.send = lax.dynamic_index_in_dim(pairs, 1 - side, 1, False).astype(BF16)
            self.send = self.send.reshape(-1, cols)
            self.mine = lax.dynamic_index_in_dim(pairs, side, 1, False).reshape(-1, cols)


def on_device(
    h_fwd,
    h_rc,
    tokens,
    loss_mask,
    species,
    w_in,
    a_log,
    dt_bias,
    d_skip,
    norm_gain,
    w_out,
    final_gain,
    w_head,
    log_var,
):
    length, width = h_fwd.shape[1], h_fwd.shape[2]
    vocab, kinds = w_head.shape[0], log_var.shape[0]
    ctx = lax.axis_size("ctx")
    bits = bits_of("ctx")
    rows = 2
    flat = rows * length

    bias, alog, skip = dt_bias[None], a_log[None], d_skip[None]
    win_t = w_in.T
    gain, final, kind = norm_gain[None], final_gain[None], species[None]
    head = jnp.concatenate([w_head, jnp.zeros((8 - vocab, width), F32)], axis=0)

    state_shape = (rows, 2, STATE, INNER)
    wide = ((length, INNER), BF16)
    full = (rows, length, INNER)
    proj, total, small = call(
        front_kernel,
        "front",
        [
            (h_fwd, "all hbm"),
            (h_rc, "all hbm"),
            (win_t, "all hbm"),
            (bias, "all"),
            (alog, "all"),
            (loss_mask, "all"),
            (kind, "all"),
        ],
        [
            ((rows, length, w_in.shape[1]), BF16, "row hbm"),
            (state_shape, BF16, "row"),
            ((rows + 1, 1, INNER), F32, "all"),
        ],
        [wide, wide],
        cost(2e9, 7e6),
    )
    left_own, right_own = call(
        local_kernel,
        "local",
        [(proj, "row hbm"), (bias, "all"), (alog, "all"), (skip, "all")],
        [(full, F32, "row hbm"), (full, F32, "row hbm")],
        (),
        cost(4e9, 4e6),
    )
    carry, rounds, counts = scan_states(total, small)
    out_left, out_right, nsum, res, sent = call(
        out_kernel,
        "out",
        [
            (proj, "row hbm"),
            (carry, "row"),
            (left_own, "row hbm"),
            (right_own, "row hbm"),
            (h_fwd, "all hbm"),
            (h_rc, "all hbm"),
            (bias, "all"),
            (alog, "all"),
            (gain, "all"),
            (w_out, "all hbm"),
            (final, "all"),
            (head, "all"),
            (tokens, "all"),
            (loss_mask, "all"),
        ],
        [
            (full, F32, "row hbm"),
            (full, F32, "row hbm"),
            ((flat, INNER), BF16, "half"),
            ((rows, length, width), F32, "row hbm"),
            ((24, length), F32, "all"),
        ],
        (),
        cost(2e9, 8e6),
    )

    sent, counts = together(sent, counts)
    got = lax.ppermute(sent, "ctx", [(i, ctx - 1 - i) for i in range(ctx)])
    for bit in range(bits_of("dp")):
        counts = counts + partner(counts, "dp", bit)
    ce, d_res, d_mix, d_left, d_right, d_gate, d_state = call(
        functools.partial(head_kernel, vocab=vocab, loss_scale=float(length * ctx)),
        "head",
        [
            (proj, "row hbm"),
            (sent, "all"),
            (got, "all"),
            (counts, "all"),
            (kind, "all"),
            (log_var[None], "all"),
            (res, "row hbm"),
            (out_left, "row hbm"),
            (out_right, "row hbm"),
            (bias, "all"),
            (alog, "all"),
            (gain, "all"),
            (w_out, "all hbm"),
            (final, "all"),
            (head, "all"),
        ],
        [
            ((1, length), F32, "all"),
            ((rows, length, width), F32, "row hbm"),
            ((flat, width), BF16, "half"),
            (full, BF16, "row hbm"),
            (full, BF16, "row hbm"),
            ((flat, INNER), BF16, "half"),
            (state_shape, BF16, "row"),
        ],
        [wide, wide],
        cost(2e9, 8e6),
    )
    ce_sum = Sum(ce)
    hidden = jnp.concatenate([h_fwd[0], h_rc[0]], axis=0)
    hidden_theirs = their_half(hidden)

    entering = jnp.zeros(state_shape, F32)
    early, early_got = [], []
    for bit in range(bits):
        last = bit == bits - 1
        send = to_send(d_state, bit, last)
        if bit == 1:
            send, early[0].send, early[1].send, ce_sum.array = together(
                send, early[0].send, early[1].send, ce_sum.array
            )
        elif bit > 1:
            send, ce_sum.array = together(send, ce_sum.array)
        theirs = partner(send, "ctx", bit)
        if bit == 1:
            early_got = [partner(share.send, "ctx", 0) for share in early]
        if bit > 0:
            ce_sum.step()
        if last:
            for share, got in zip(early, early_got):
                share.pass_on(got)
            theirs, early[0].send, early[1].send = together(theirs, early[0].send, early[1].send)
        d_state, entering = scan_round(d_state, entering, bit, last, rounds[bit], theirs)
        if bit == 0:
            early = [
                RowShare(nsum, their_half(nsum), d_mix),
                RowShare(hidden, hidden_theirs, d_gate),
            ]
    following = entering.astype(BF16)
    d_val, d_key, d_read, d_a, d_dt = call(
        adjoint_kernel,
        "adjoint",
        [
            (proj, "row hbm"),
            (carry, "row"),
            (d_left, "row hbm"),
            (d_right, "row hbm"),
            (bias, "all"),
            (alog, "all"),
            (skip, "all"),
        ],
        [
            (full, F32, "row hbm"),
            ((rows, length, STATE), F32, "row"),
            ((rows, length, STATE), F32, "row"),
            ((rows, length, HEADS), F32, "row"),
            ((rows, length, HEADS), F32, "row"),
        ],
        [((HEADS, length), F32), ((HEADS, length), F32), wide, wide],
        cost(8e9, 6e6),
    )
    (d_rest,) = call(
        finish_kernel,
        "finish",
        [
            (proj, "row hbm"),
            (carry, "row"),
            (following, "row"),
            (d_val, "row hbm"),
            (d_key, "row"),
            (d_read, "row"),
            (d_a, "row"),
            (d_dt, "row"),
            (bias, "all"),
            (alog, "all"),
        ],
        [((flat, INNER + 2 * STATE + HEADS), BF16, "half")],
        [wide, wide],
        cost(2e9, 5e6),
    )
    late = RowShare(hidden, hidden_theirs, d_rest)
    late.send, d_rest = together(late.send, d_rest)
    grad_fwd, grad_rc = call(
        input_kernel,
        "input",
        [(d_rest, "half"), (d_gate, "half"), (win_t, "all hbm"), (d_res, "row hbm")],
        [(h_fwd.shape, BF16, "all"), (h_rc.shape, BF16, "all")],
        (),
        cost(2e9, 7e6),
    )
    while not late.done():
        shares = [share for share in early + [late] if not share.done()]
        ce_sum.array, *sends = together(ce_sum.array, *[share.send for share in shares])
        got = [partner(send, "ctx", share.bit) for share, send in zip(shares, sends)]
        ce_sum.step()
        if late.bit == 0:
            grad_fwd, grad_rc, *got = together(grad_fwd, grad_rc, *got)
        else:
            got = together(*got)
        for share, arrived in zip(shares, got):
            share.pass_on(arrived)
    ce_sums = ce_sum.finish()[0, :kinds]
    grad_w_in = jnp.concatenate(
        [late.mine[:, :INNER], early[1].mine, late.mine[:, INNER:]], axis=1
    )
    scaled = jnp.exp(-log_var) / jnp.maximum(counts[0, 0, :kinds], 1.0)
    loss = jnp.sum(scaled * ce_sums + log_var).reshape(1)
    grad_log_var = 1.0 - scaled * ce_sums
    return (loss, grad_log_var, grad_fwd, grad_rc, grad_w_in, early[0].mine)


def solution(mesh):
    return jax.shard_map(
        on_device,
        mesh=mesh,
        in_specs=(
            P(("groups", "dp"), "ctx", None),
            P(("groups", "dp"), "ctx", None),
            P(("groups", "dp"), "ctx"),
            P(("groups", "dp"), "ctx"),
            P(("groups", "dp")),
            P(),
            P(),
            P(),
            P(),
            P(),
            P(),
            P(),
            P(),
            P(),
        ),
        out_specs=(
            P("groups"),
            P("groups"),
            P(("groups", "dp"), "ctx", None),
            P(("groups", "dp"), "ctx", None),
            P(("groups", "dp", "ctx"), None),
            P(("groups", "dp", "ctx"), None),
        ),
        check_vma=False,
    )
```

```python
import functools

import jax
import jax.numpy as jnp
from jax import lax
from jax.experimental import pallas as pl
from jax.experimental.pallas import tpu as pltpu
from jax.sharding import PartitionSpec as P

HEADS = 16
HEAD_DIM = 64
STATE = 64
INNER = HEADS * HEAD_DIM
PAIRS = HEADS // 2
LANES = 2 * HEAD_DIM
USED = INNER + 2 * STATE + HEADS
REST = (USED + 127) // 128 * 128
EPSILON = 1e-05

F32 = jnp.float32
BF16 = jnp.bfloat16
HIGH = lax.Precision.HIGHEST
VMEM_BYTES = 14 * 1024 * 1024


def mm(a, b, ca=1, cb=0, precision=None):
    return lax.dot_general(
        a, b, (((ca,), (cb,)), ((), ())), precision=precision, preferred_element_type=F32
    )


def iota(shape, dim):
    return lax.broadcasted_iota(jnp.int32, shape, dim)


def pair_wide(x, j):
    first = iota((x.shape[0], LANES), 1) < HEAD_DIM
    return jnp.where(first, x[:, 2 * j : 2 * j + 1], x[:, 2 * j + 1 : 2 * j + 2])


def lanes_of(j):
    return slice(j * LANES, (j + 1) * LANES)


def softplus(x):
    return jnp.maximum(x, 0.0) + jnp.log1p(jnp.exp(-jnp.abs(x)))


def tri(length, kind):
    rows, cols = iota((length, length), 0), iota((length, length), 1)
    return jnp.where(rows >= cols if kind == "ge" else rows > cols, 1.0, 0.0).astype(F32)


def head_sum(x):
    pick = (iota((INNER, HEADS), 0) // HEAD_DIM == iota((INNER, HEADS), 1)).astype(F32).astype(BF16)
    return mm(x.astype(BF16), pick)


def steps(proj_ref, bias_ref, alog_ref, row=0):
    raw = proj_ref[row, :, 2 * INNER + 2 * STATE :].astype(F32) + bias_ref[...]
    dt = softplus(raw)
    a = -jnp.exp(alog_ref[...]) * dt
    cum = mm(tri(a.shape[0], "ge"), a, precision=HIGH)
    return raw, dt, a, cum, cum - a, cum[-1:, :]


def turned(x):
    n = x.shape[0]
    eye = jnp.where(iota((n, n), 0) == iota((n, n), 1), 1.0, 0.0).astype(F32)
    return mm(x, eye, 0, 0, HIGH)


def turned_back(x):
    n = x.shape[0]
    eye = jnp.where(iota((n, n), 0) == iota((n, n), 1), 1.0, 0.0).astype(F32)
    return mm(x, eye, 0, 0, HIGH)


def keys_of(proj_ref):
    return proj_ref[0, :, 2 * INNER : 2 * INNER + STATE]


def reads_of(proj_ref):
    return proj_ref[0, :, 2 * INNER + STATE : 2 * INNER + 2 * STATE]


def front_kernel(
    fwd_ref,
    rc_ref,
    win_hbm,
    bias_ref,
    alog_ref,
    mask_ref,
    species_ref,
    proj_ref,
    total_ref,
    small_ref,
    win,
    wide_l,
    wide_r,
    arrived,
    *,
    cuts,
):
    copies = [
        pltpu.make_async_copy(
            win_hbm.at[pl.ds(low, high - low)], win.at[pl.ds(low, high - low)], arrived.at[i]
        )
        for i, (low, high) in enumerate(zip(cuts, cuts[1:]))
    ]
    for copy in copies:
        copy.start()
    hidden = jnp.concatenate([fwd_ref[0], rc_ref[0]], axis=0)
    n = fwd_ref.shape[1]
    for copy, low, high in zip(copies, cuts, cuts[1:]):
        copy.wait()
        part = mm(hidden, win[low:high, :], 1, 1).astype(BF16)
        proj_ref[0, :, low:high] = part[:n]
        proj_ref[1, :, low:high] = part[n:]
    for row in range(2):
        unused, dt, a, cum, cex, tot = steps(proj_ref, bias_ref, alog_ref, row)
        w_l = jnp.exp(tot - cum) * dt
        w_r = jnp.exp(cex) * dt
        block = jnp.exp(tot)
        for j in range(PAIRS):
            s = lanes_of(j)
            v = proj_ref[row, :, s].astype(F32)
            wide_l[:, s] = (v * pair_wide(w_l, j)).astype(BF16)
            wide_r[:, s] = (v * pair_wide(w_r, j)).astype(BF16)
            small_ref[row, :, s] = pair_wide(block, j)
        keys = proj_ref[row, :, 2 * INNER : 2 * INNER + STATE]
        total_ref[row, 0] = mm(keys, wide_l[...], 0, 0).astype(BF16)
        total_ref[row, 1] = mm(keys, wide_r[...], 0, 0).astype(BF16)
    scored = jnp.sum(mask_ref[...].astype(F32), axis=1, keepdims=True)
    small_ref[2] = jnp.where(iota((1, INNER), 1) == species_ref[0, 0], scored, 0.0)


def local_kernel(proj_ref, bias_ref, alog_ref, skip_ref, left_ref, right_ref):
    unused, dt, a, cum, cex, tot = steps(proj_ref, bias_ref, alog_ref)
    n = cum.shape[0]
    cum_t, cex_t, dt_t = turned(cum), turned(cex), turned(dt)
    score = mm(reads_of(proj_ref), keys_of(proj_ref), 1, 1)
    t, s = iota((n, n), 0), iota((n, n), 1)
    first = iota((n, LANES), 1) < HEAD_DIM
    zero = jnp.zeros((n, LANES), BF16)
    for j in range(PAIRS):
        lanes = lanes_of(j)
        v = proj_ref[0, :, lanes]
        left, right = [], []
        for h in (2 * j, 2 * j + 1):
            gap = jnp.where(
                t >= s,
                cum[:, h : h + 1] - cum_t[h : h + 1, :],
                cex_t[h : h + 1, :] - cex[:, h : h + 1],
            )
            mix = jnp.exp(jnp.minimum(gap, 0.0)) * score * dt_t[h : h + 1, :]
            left.append(jnp.where(t >= s, mix, 0.0).astype(BF16))
            right.append(jnp.where(t <= s, mix, 0.0).astype(BF16))
        stacked = jnp.concatenate([jnp.where(first, v, zero), jnp.where(first, zero, v)], axis=0)
        skip = pair_wide(skip_ref[...], j) * v.astype(F32)
        left_ref[0, :, lanes] = (mm(jnp.concatenate(left, axis=1), stacked) + skip).astype(BF16)
        right_ref[0, :, lanes] = (mm(jnp.concatenate(right, axis=1), stacked) + skip).astype(BF16)


def out_kernel(
    proj_ref,
    carry_ref,
    left_in,
    right_in,
    fwd_ref,
    rc_ref,
    bias_ref,
    alog_ref,
    gain_ref,
    wout_ref,
    final_ref,
    head_ref,
    token_ref,
    mask_ref,
    left_ref,
    right_ref,
    nsum_ref,
    res_ref,
    sent_ref,
):
    row = pl.program_id(0)
    unused, dt, a, cum, cex, tot = steps(proj_ref, bias_ref, alog_ref)
    e_l, e_r = jnp.exp(cum), jnp.exp(tot - cex)
    reads = reads_of(proj_ref)
    from_l = mm(reads, carry_ref[0, 0])
    from_r = mm(reads, carry_ref[0, 1])
    for j in range(PAIRS):
        s = lanes_of(j)
        out_l = left_in[0, :, s].astype(F32) + pair_wide(e_l, j) * from_l[:, s]
        out_r = right_in[0, :, s].astype(F32) + pair_wide(e_r, j) * from_r[:, s]
        left_ref[0, :, s] = out_l.astype(BF16)
        right_ref[0, :, s] = out_r.astype(BF16)
    gate = proj_ref[0, :, INNER : 2 * INNER].astype(F32)
    gated = gate * jax.nn.sigmoid(gate)
    u_l = left_ref[0].astype(F32) * gated
    u_r = right_ref[0].astype(F32) * gated
    k_l = lax.rsqrt(jnp.mean(u_l * u_l, axis=1, keepdims=True) + EPSILON)
    k_r = lax.rsqrt(jnp.mean(u_r * u_r, axis=1, keepdims=True) + EPSILON)
    nsum = ((u_l * k_l + u_r * k_r) * gain_ref[...]).astype(BF16)
    nsum_ref[...] = nsum
    hidden = jnp.where(row == 0, fwd_ref[0], rc_ref[0])
    res = hidden.astype(F32) + mm(nsum, wout_ref[...])
    res_ref[0] = res
    normed = res * lax.rsqrt(jnp.mean(res * res, axis=1, keepdims=True) + EPSILON) * final_ref[...]
    sent_ref[pl.ds(row * 8, 8), :] = mm(head_ref[...], normed, 1, 1, HIGH)

    @pl.when(row == 0)
    def _():
        line = iota((8, normed.shape[0]), 0)
        sent_ref[16:24, :] = jnp.where(
            line == 0,
            token_ref[...].astype(F32),
            jnp.where(line == 1, mask_ref[...].astype(F32), 0.0),
        )


def head_kernel(
    proj_ref,
    sent_ref,
    got_ref,
    counts_ref,
    their_counts_ref,
    species_ref,
    logvar_ref,
    res_ref,
    left_ref,
    right_ref,
    bias_ref,
    alog_ref,
    gain_ref,
    wout_ref,
    final_ref,
    head_ref,
    ce_ref,
    dcot_ref,
    dleft_ref,
    dright_ref,
    dstate_ref,
    wide_l,
    wide_r,
    *,
    vocab,
    loss_scale,
):
    row = pl.program_id(0)
    n = sent_ref.shape[1]
    mirror = jnp.where(iota((n, n), 0) + iota((n, n), 1) == n - 1, 1.0, 0.0).astype(F32)
    to, of = iota((8, 8), 0), iota((8, 8), 1)
    swap = jnp.where(jnp.where(to < 4, 3 - to, to) == of, 1.0, 0.0).astype(F32)
    other = mm(got_ref[pl.ds((1 - row) * 8, 8), :], mirror, precision=HIGH)
    total = sent_ref[pl.ds(row * 8, 8), :] + mm(swap, other, precision=HIGH)
    seen = mm(got_ref[16:24, :], mirror, precision=HIGH)
    their_token = jnp.where(seen[0:1] < 4.0, 3.0 - seen[0:1], seen[0:1])
    token = jnp.where(row == 0, sent_ref[16:17, :], their_token)
    mask = jnp.where(row == 0, sent_ref[17:18, :], seen[1:2])
    kinds = logvar_ref.shape[1]
    scaled = jnp.exp(-logvar_ref[...]) / jnp.maximum(
        counts_ref[0, :, :kinds] + their_counts_ref[0, :, :kinds], 1.0
    )
    chosen = iota((1, kinds), 1) == species_ref[...]
    weight = loss_scale * mask * jnp.sum(jnp.where(chosen, scaled, 0.0), axis=1, keepdims=True)
    which = iota(total.shape, 0)
    powers = jnp.where(which < vocab, jnp.exp(total), 0.0)
    expsum = jnp.sum(powers, axis=0, keepdims=True)
    hot = jnp.where(which.astype(F32) == token, 1.0, 0.0)

    @pl.when(row == 0)
    def _():
        ce = mask * (jnp.log(expsum) - jnp.sum(total * hot, axis=0, keepdims=True))
        ce = jnp.sum(ce, axis=1, keepdims=True)
        ce_ref[...] = jnp.where(iota((1, n), 1) == species_ref[...], ce, 0.0)

    d_logit = weight * (powers / expsum - hot)
    d_normed = mm(d_logit, head_ref[...], 0, 0, HIGH) * final_ref[...]
    res = res_ref[0]
    k = lax.rsqrt(jnp.mean(res * res, axis=1, keepdims=True) + EPSILON)
    d_res = k * (d_normed - res * (k * k * jnp.mean(d_normed * res, axis=1, keepdims=True)))
    d_mix = d_res.astype(BF16)
    dcot_ref[:, :INNER] = d_mix
    d_sum = mm(d_mix, wout_ref[...], 1, 1) * gain_ref[...]
    gate = proj_ref[0, :, INNER : 2 * INNER].astype(F32)
    sig = jax.nn.sigmoid(gate)
    gated = gate * sig
    d_gated = jnp.zeros_like(gate)
    for source, target in ((left_ref, dleft_ref), (right_ref, dright_ref)):
        out = source[0].astype(F32)
        u = out * gated
        k = lax.rsqrt(jnp.mean(u * u, axis=1, keepdims=True) + EPSILON)
        d_u = k * (d_sum - u * (k * k * jnp.mean(d_sum * u, axis=1, keepdims=True)))
        target[0] = (d_u * gated).astype(BF16)
        d_gated = d_gated + d_u * out
    dcot_ref[:, INNER:] = (d_gated * (sig + gated * (1.0 - sig))).astype(BF16)
    unused, dt, a, cum, cex, tot = steps(proj_ref, bias_ref, alog_ref)
    e_l, e_r = jnp.exp(cum), jnp.exp(tot - cex)
    for j in range(PAIRS):
        s = lanes_of(j)
        wide_l[:, s] = (dleft_ref[0, :, s].astype(F32) * pair_wide(e_l, j)).astype(BF16)
        wide_r[:, s] = (dright_ref[0, :, s].astype(F32) * pair_wide(e_r, j)).astype(BF16)
    reads = reads_of(proj_ref)
    dstate_ref[0, 1] = mm(reads, wide_l[...], 0, 0).astype(BF16)
    dstate_ref[0, 0] = mm(reads, wide_r[...], 0, 0).astype(BF16)


def adjoint_kernel(
    proj_ref,
    carry_ref,
    dleft_ref,
    dright_ref,
    bias_ref,
    alog_ref,
    skip_ref,
    dval_ref,
    dkey_ref,
    dread_ref,
    da_ref,
    ddt_ref,
    cols_l,
    cols_r,
    wide_l,
    wide_r,
):
    unused, dt, a, cum, cex, tot = steps(proj_ref, bias_ref, alog_ref)
    n = cum.shape[0]
    cum_t, cex_t = turned(cum), turned(cex)
    keys, reads = keys_of(proj_ref), reads_of(proj_ref)
    score = mm(keys, reads, 1, 1)
    s, t = iota((n, n), 0), iota((n, n), 1)
    first = iota((n, LANES), 1) < HEAD_DIM
    zero = jnp.zeros((n, LANES), BF16)
    d_score = jnp.zeros((n, n), F32)
    row_h = jnp.zeros((n, LANES), F32)
    row_l = jnp.zeros((n, LANES), F32)
    row_r = jnp.zeros((n, LANES), F32)
    e_l, e_r = jnp.exp(cum), jnp.exp(tot - cex)
    for j in range(PAIRS):
        lanes = lanes_of(j)
        v = proj_ref[0, :, lanes]
        d_l, d_r = dleft_ref[0, :, lanes], dright_ref[0, :, lanes]
        v_split = jnp.concatenate([jnp.where(first, v, zero), jnp.where(first, zero, v)], axis=0)
        d_mix = mm(v_split, jnp.concatenate([d_l, d_r], axis=0), 1, 1)
        mixes, sums_h, sums_l, sums_r = [], [], [], []
        for i, h in enumerate((2 * j, 2 * j + 1)):
            gap = jnp.where(
                t >= s,
                cum_t[h : h + 1, :] - cum[:, h : h + 1],
                cex[:, h : h + 1] - cex_t[h : h + 1, :],
            )
            decay = jnp.exp(jnp.minimum(gap, 0.0))
            step = dt[:, h : h + 1]
            d_l_mix = d_mix[i * n : (i + 1) * n, :n]
            d_r_mix = d_mix[i * n : (i + 1) * n, n:]
            scaled = decay * (
                jnp.where(t >= s, d_l_mix, 0.0) + jnp.where(t <= s, d_r_mix, 0.0)
            )
            with_step = scaled * step
            d_score = d_score + with_step
            flow = with_step * score
            flow_l = jnp.where(t > s, flow, 0.0)
            flow_r = jnp.where(t < s, flow, 0.0)
            cols_l[h : h + 1, :] = jnp.sum(flow_l, axis=0, keepdims=True)
            cols_r[h : h + 1, :] = jnp.sum(flow_r, axis=0, keepdims=True)
            sums_h.append((scaled * score).astype(BF16))
            sums_l.append(flow_l.astype(BF16))
            sums_r.append(flow_r.astype(BF16))
            mix = decay * score * step
            mixes.append(jnp.where(t >= s, mix, 0.0).astype(BF16))
            mixes.append(jnp.where(t <= s, mix, 0.0).astype(BF16))
        pick_rows, pick_cols = iota((2 * n, LANES), 0), iota((2 * n, LANES), 1)
        pick = (
            jnp.where(pick_cols == 2 * j + (pick_rows >= n).astype(jnp.int32), 1.0, 0.0)
            .astype(F32)
            .astype(BF16)
        )
        row_h = row_h + mm(jnp.concatenate(sums_h, axis=1), pick)
        row_l = row_l + mm(jnp.concatenate(sums_l, axis=1), pick)
        row_r = row_r + mm(jnp.concatenate(sums_r, axis=1), pick)
        d_split = jnp.concatenate(
            [
                jnp.where(first, d_l, zero),
                jnp.where(first, d_r, zero),
                jnp.where(first, zero, d_l),
                jnp.where(first, zero, d_r),
            ],
            axis=0,
        )
        both = d_l.astype(F32) + d_r.astype(F32)
        dval_ref[0, :, lanes] = (
            mm(jnp.concatenate(mixes, axis=1), d_split) + pair_wide(skip_ref[...], j) * both
        ).astype(BF16)
        wide_l[:, lanes] = (d_l.astype(F32) * pair_wide(e_l, j)).astype(BF16)
        wide_r[:, lanes] = (d_r.astype(F32) * pair_wide(e_r, j)).astype(BF16)
    carry_l, carry_r = carry_ref[0, 0], carry_ref[0, 1]
    d_score_b = d_score.astype(BF16)
    dkey_ref[0] = mm(d_score_b, reads)
    dread_ref[0] = (
        mm(d_score_b, keys, 0, 0)
        + mm(wide_l[...], carry_l, 1, 1)
        + mm(wide_r[...], carry_r, 1, 1)
    )
    d_cum = (
        head_sum(wide_l[...].astype(F32) * mm(reads, carry_l))
        + turned_back(cols_l[...])
        - row_l[:, :HEADS]
    )
    d_rcum = head_sum(wide_r[...].astype(F32) * mm(reads, carry_r))
    d_cex = row_r[:, :HEADS] - turned_back(cols_r[...])
    ge, gt = tri(n, "ge"), tri(n, "gt")
    da_ref[0] = mm(ge, d_cum, 0, 0, HIGH) + mm(gt, d_cex, 0, 0, HIGH) + mm(ge, d_rcum, 1, 0, HIGH)
    ddt_ref[0] = row_h[:, :HEADS]


def finish_kernel(
    proj_ref,
    carry_ref,
    next_ref,
    dval_in,
    dkey_in,
    dread_in,
    da_in,
    ddt_in,
    bias_ref,
    alog_ref,
    dproj_ref,
    wide_l,
    wide_r,
):
    raw, dt, a, cum, cex, tot = steps(proj_ref, bias_ref, alog_ref)
    keys = keys_of(proj_ref)
    f_l, f_r = jnp.exp(tot - cum), jnp.exp(cex)
    w_l, w_r = f_l * dt, f_r * dt
    next_r, next_l = next_ref[0, 0], next_ref[0, 1]
    z_l, z_r = mm(keys, next_l), mm(keys, next_r)
    for j in range(PAIRS):
        s = lanes_of(j)
        v = proj_ref[0, :, s].astype(F32)
        wide_w_l, wide_w_r = pair_wide(w_l, j), pair_wide(w_r, j)
        dproj_ref[:, s] = (
            dval_in[0, :, s].astype(F32) + wide_w_l * z_l[:, s] + wide_w_r * z_r[:, s]
        ).astype(BF16)
        wide_l[:, s] = (v * wide_w_l).astype(BF16)
        wide_r[:, s] = (v * wide_w_r).astype(BF16)
    values = proj_ref[0, :, :INNER].astype(F32)
    dw_l, dw_r = head_sum(values * z_l), head_sum(values * z_r)
    d_key = dkey_in[0] + mm(wide_l[...], next_l, 1, 1) + mm(wide_r[...], next_r, 1, 1)
    dproj_ref[:, INNER : INNER + STATE] = d_key.astype(BF16)
    dproj_ref[:, INNER + STATE : INNER + 2 * STATE] = dread_in[0].astype(BF16)
    through = jnp.sum(
        next_l.astype(F32) * carry_ref[0, 0].astype(F32)
        + next_r.astype(F32) * carry_ref[0, 1].astype(F32),
        axis=0,
        keepdims=True,
    )
    through = head_sum(jnp.broadcast_to(through, (8, INNER)))[:1]
    q_l, q_r = dw_l * w_l, dw_r * w_r
    n = cum.shape[0]
    ge, gt = tri(n, "ge"), tri(n, "gt")
    d_tot = jnp.exp(tot) * through + jnp.sum(q_l, axis=0, keepdims=True)
    d_a = da_in[0] + mm(gt, q_r, 0, 0, HIGH) - mm(ge, q_l, 0, 0, HIGH) + d_tot
    d_dt = ddt_in[0] + dw_l * f_l + dw_r * f_r - d_a * jnp.exp(alog_ref[...])
    d_raw = d_dt * jax.nn.sigmoid(raw)
    dproj_ref[:, INNER + 2 * STATE :] = jnp.zeros((n, REST - INNER - 2 * STATE), BF16)
    dproj_ref[:, INNER + 2 * STATE : INNER + 2 * STATE + HEADS] = d_raw.astype(BF16)


def input_kernel(rest_ref, cot_ref, win_ref, fwd_ref, rc_ref):
    row = pl.program_id(0)
    grad = (
        cot_ref[:, :INNER].astype(F32)
        + mm(cot_ref[:, INNER:], win_ref[INNER : 2 * INNER])
        + mm(rest_ref[:, :INNER], win_ref[:INNER])
        + mm(rest_ref[:, INNER:USED], win_ref[2 * INNER :])
    ).astype(BF16)

    @pl.when(row == 0)
    def _():
        fwd_ref[0] = grad

    @pl.when(row == 1)
    def _():
        rc_ref[0] = grad


def weight_kernel(place_ref, *refs, block, widths):
    rows, theirs = refs[: len(widths)], refs[len(widths) : 2 * len(widths)]
    cot_ref, their_cot_ref, send_ref, keep_ref, both = refs[2 * len(widths) :]
    at = 0
    for rows_ref, their_rows_ref, width in zip(rows, theirs, widths):
        half = their_rows_ref.shape[1]
        mine = jnp.where(place_ref[0] == 0, rows_ref[:, :half], rows_ref[:, half:])
        cols = slice(at, at + width)
        both[:, cols] = mm(mine, cot_ref[:, cols], 0, 0) + mm(
            their_rows_ref[...], their_cot_ref[:, cols], 0, 0
        )
        at += width
    side = place_ref[1]
    for i in range(keep_ref.shape[0] // block):
        here = slice(i * block, (i + 1) * block)
        keep_ref[here, :] = both[pl.ds((2 * i + side) * block, block), :]
        send_ref[here, :] = both[pl.ds((2 * i + 1 - side) * block, block), :].astype(BF16)


def halve_kernel(side_ref, mine_ref, got_ref, send_ref, keep_ref, *, block):
    side = side_ref[0]
    for i in range(keep_ref.shape[0] // block):
        here = slice(i * block, (i + 1) * block)
        kept, sent = pl.ds((2 * i + side) * block, block), pl.ds((2 * i + 1 - side) * block, block)
        keep_ref[here, :] = mine_ref[kept, :] + got_ref[kept, :].astype(F32)
        send_ref[here, :] = (mine_ref[sent, :] + got_ref[sent, :].astype(F32)).astype(BF16)


def by_row(shape):
    rest = (0,) * (len(shape) - 1)
    return pl.BlockSpec((1,) + tuple(shape[1:]), lambda g: (g,) + rest)


def by_half(shape):
    return pl.BlockSpec((shape[0] // 2, shape[1]), lambda g: (g, 0))


def whole(shape):
    zeros = (0,) * len(shape)
    return pl.BlockSpec(tuple(shape), lambda g: zeros)


FAR = ("row hbm", "half hbm", "all hbm")


def far(array):
    return pltpu.with_memory_space_constraint(array, pltpu.HBM)


def placed(shape, dtype, kind):
    return pltpu.HBM(shape, dtype) if kind in FAR else jax.ShapeDtypeStruct(shape, dtype)


def call(kernel, name, operands, results, scratch=(), cost=None):
    specs = {"row": by_row, "half": by_half, "all": whole}
    specs.update({kind + " hbm": spec for kind, spec in list(specs.items())})
    return pl.pallas_call(
        kernel,
        name=name,
        grid=(2,),
        in_specs=[specs[kind](array.shape) for array, kind in operands],
        out_specs=[specs[kind](shape) for shape, dtype, kind in results],
        out_shape=[placed(shape, dtype, kind) for shape, dtype, kind in results],
        scratch_shapes=[pltpu.VMEM(shape, dtype) for shape, dtype in scratch],
        compiler_params=pltpu.CompilerParams(
            dimension_semantics=("arbitrary",), vmem_limit_bytes=VMEM_BYTES
        ),
        cost_estimate=cost,
    )(*[far(array) if kind in FAR else array for array, kind in operands])


def cost(flops, moved):
    return pl.CostEstimate(flops=int(flops), transcendentals=0, bytes_accessed=int(moved))


def bits_of(axis):
    return lax.axis_size(axis).bit_length() - 1


def partner(array, axis, bit):
    return lax.ppermute(array, axis, [(i, i ^ (1 << bit)) for i in range(lax.axis_size(axis))])


def together(*arrays):
    return lax.optimization_barrier(arrays)


class Sum:
    def __init__(self, array):
        self.array = array
        self.left = [("ctx", bit) for bit in range(bits_of("ctx"))]
        self.left += [("dp", bit) for bit in range(bits_of("dp"))]

    def step(self):
        if self.left:
            axis, bit = self.left.pop(0)
            self.array = self.array + partner(self.array, axis, bit)

    def finish(self):
        while self.left:
            self.step()
        return self.array


def is_upper(bit):
    return ((lax.axis_index("ctx") >> bit) & 1) == 1


def factors(upper, lead_l, lead_r, decay, theirs):
    one, zero = jnp.ones_like(decay), jnp.zeros_like(decay)
    into = jnp.stack([jnp.where(upper, lead_l, zero), jnp.where(upper, zero, lead_r)], axis=1)
    keep = jnp.stack([jnp.where(upper, one, theirs), jnp.where(upper, theirs, one)], axis=1)
    take = jnp.stack([jnp.where(upper, decay, one), jnp.where(upper, one, decay)], axis=1)
    return into, keep, take


def scan_round(total, entering, bit, last, into_keep_take, theirs):
    into, keep, take = into_keep_take
    theirs = theirs.astype(F32)
    if last:
        return None, entering + into * theirs[:, None]
    return (
        (keep * total.astype(F32) + take * theirs).astype(BF16),
        entering + into * theirs,
    )


def to_send(total, bit, last):
    return jnp.where(is_upper(bit), total[:, 1], total[:, 0]) if last else total


def scan_states(total, small):
    bits = bits_of("ctx")
    entering = jnp.zeros(total.shape, F32)
    rows = total.shape[0]
    lead_l = jnp.ones((rows, 1, INNER), F32)
    lead_r = lead_l
    rounds = []
    for bit in range(bits):
        last, upper = bit == bits - 1, is_upper(bit)
        sent, small = together(to_send(total, bit, last), small)
        theirs = partner(sent, "ctx", bit)
        theirs_small = partner(small, "ctx", bit)
        decay, their_decay = small[:rows], theirs_small[:rows]
        rounds.append(factors(upper, lead_l, lead_r, decay, their_decay))
        total, entering = scan_round(total, entering, bit, last, rounds[-1], theirs)
        lead_l = jnp.where(upper, lead_l * their_decay, lead_l)
        lead_r = jnp.where(upper, lead_r, lead_r * their_decay)
        small = jnp.concatenate([decay * their_decay, small[rows:] + theirs_small[rows:]], axis=0)
    return entering.astype(BF16), rounds, small[rows:]


def over_cores(array):
    return lax.ppermute(array, "dp", [(0, 1), (1, 0)])


def their_half(rows_of):
    half = rows_of.shape[1] // 2
    return over_cores(
        jnp.where(lax.axis_index("dp") == 0, rows_of[:, half:], rows_of[:, :half])
    )


class RowShare:
    def __init__(self, rows_of, theirs, cotangent):
        ctx = lax.axis_size("ctx")
        their_cot = over_cores(cotangent)
        place = jnp.stack([lax.axis_index("dp"), lax.axis_index("ctx") & 1]).astype(jnp.int32)
        half, cols = theirs[0].shape[1], cotangent.shape[1]
        block = half // ctx
        vmem = pl.BlockSpec(memory_space=pltpu.VMEM)
        self.send, self.mine = pl.pallas_call(
            functools.partial(
                weight_kernel, block=block, widths=(cols // len(rows_of),) * len(rows_of)
            ),
            name="weight",
            in_specs=[pl.BlockSpec(memory_space=pltpu.SMEM)] + [vmem] * (2 * len(rows_of) + 2),
            out_specs=[vmem, vmem],
            out_shape=[
                jax.ShapeDtypeStruct((half // 2, cols), BF16),
                jax.ShapeDtypeStruct((half // 2, cols), F32),
            ],
            scratch_shapes=[pltpu.VMEM((half, cols), F32)],
            compiler_params=pltpu.CompilerParams(vmem_limit_bytes=VMEM_BYTES),
            cost_estimate=cost(1.2e9, 6e6),
        )(place, *rows_of, *theirs, cotangent, their_cot)
        self.bit = 0
        self.bits = bits_of("ctx")
        self.block = block

    def done(self):
        return self.bit == self.bits

    def pass_on(self, got):
        self.bit += 1
        if self.done():
            self.mine = self.mine + got.astype(F32)
            return
        rows, cols = self.mine.shape
        side = ((lax.axis_index("ctx") >> self.bit) & 1).astype(jnp.int32).reshape(1)
        self.send, self.mine = pl.pallas_call(
            functools.partial(halve_kernel, block=self.block),
            name="halve",
            grid=(1,),
            in_specs=[pl.BlockSpec(memory_space=pltpu.SMEM), whole((rows, cols)), whole((rows, cols))],
            out_specs=[whole((rows // 2, cols))] * 2,
            out_shape=[
                jax.ShapeDtypeStruct((rows // 2, cols), BF16),
                jax.ShapeDtypeStruct((rows // 2, cols), F32),
            ],
            compiler_params=pltpu.CompilerParams(vmem_limit_bytes=VMEM_BYTES),
            cost_estimate=cost(1e6, 3e6),
        )(side, self.mine, got)


def on_device(
    h_fwd,
    h_rc,
    tokens,
    loss_mask,
    species,
    w_in,
    a_log,
    dt_bias,
    d_skip,
    norm_gain,
    w_out,
    final_gain,
    w_head,
    log_var,
):
    length, width = h_fwd.shape[1], h_fwd.shape[2]
    vocab, kinds = w_head.shape[0], log_var.shape[0]
    ctx = lax.axis_size("ctx")
    bits = bits_of("ctx")
    rows = 2
    flat = rows * length

    bias, alog, skip = dt_bias[None], a_log[None], d_skip[None]
    win_t = w_in.T
    gain, final, kind = norm_gain[None], final_gain[None], species[None]
    head = jnp.concatenate([w_head, jnp.zeros((8 - vocab, width), F32)], axis=0)

    state_shape = (rows, 2, STATE, INNER)
    wide = ((length, INNER), BF16)
    full = (rows, length, INNER)
    columns = w_in.shape[1]
    cuts = [0, INNER // 2, INNER, 3 * INNER // 2, columns]
    proj, total, small = pl.pallas_call(
        functools.partial(front_kernel, cuts=cuts),
        name="front",
        grid=(1,),
        in_specs=[
            whole(h_fwd.shape),
            whole(h_rc.shape),
            pl.BlockSpec(memory_space=pltpu.HBM),
            whole(bias.shape),
            whole(alog.shape),
            whole(loss_mask.shape),
            pl.BlockSpec(memory_space=pltpu.SMEM),
        ],
        out_specs=[
            whole((rows, length, columns)),
            whole(state_shape),
            whole((rows + 1, 1, INNER)),
        ],
        out_shape=[
            pltpu.HBM((rows, length, columns), BF16),
            jax.ShapeDtypeStruct(state_shape, BF16),
            jax.ShapeDtypeStruct((rows + 1, 1, INNER), F32),
        ],
        scratch_shapes=[
            pltpu.VMEM((columns, width), BF16),
            pltpu.VMEM(*wide),
            pltpu.VMEM(*wide),
            pltpu.SemaphoreType.DMA((len(cuts) - 1,)),
        ],
        compiler_params=pltpu.CompilerParams(vmem_limit_bytes=VMEM_BYTES),
        cost_estimate=cost(2e9, 7e6),
    )(far(h_fwd), far(h_rc), far(win_t), far(bias), far(alog), far(loss_mask), kind)
    left_own, right_own = call(
        local_kernel,
        "local",
        [(proj, "row hbm"), (bias, "all"), (alog, "all"), (skip, "all")],
        [(full, BF16, "row hbm"), (full, BF16, "row hbm")],
        (),
        cost(4e9, 4e6),
    )
    carry, rounds, counts = scan_states(total, small)
    out_left, out_right, nsum, res, sent = call(
        out_kernel,
        "out",
        [
            (proj, "row hbm"),
            (carry, "row"),
            (left_own, "row hbm"),
            (right_own, "row hbm"),
            (h_fwd, "all hbm"),
            (h_rc, "all hbm"),
            (bias, "all"),
            (alog, "all"),
            (gain, "all"),
            (w_out, "all"),
            (final, "all"),
            (head, "all"),
            (tokens, "all"),
            (loss_mask, "all"),
        ],
        [
            (full, BF16, "row"),
            (full, BF16, "row"),
            ((flat, INNER), BF16, "half"),
            ((rows, length, width), F32, "row"),
            ((24, length), F32, "all"),
        ],
        (),
        cost(2e9, 8e6),
    )

    sent, counts = together(sent, counts)
    got = lax.ppermute(sent, "ctx", [(i, ctx - 1 - i) for i in range(ctx)])
    their_counts = over_cores(counts)
    ce, d_cot, d_left, d_right, d_state = call(
        functools.partial(head_kernel, vocab=vocab, loss_scale=float(length * ctx)),
        "head",
        [
            (proj, "row hbm"),
            (sent, "all"),
            (got, "all"),
            (counts, "all"),
            (their_counts, "all"),
            (kind, "all"),
            (log_var[None], "all"),
            (res, "row"),
            (out_left, "row"),
            (out_right, "row"),
            (bias, "all"),
            (alog, "all"),
            (gain, "all"),
            (w_out, "all hbm"),
            (final, "all"),
            (head, "all"),
        ],
        [
            ((1, length), F32, "all"),
            ((flat, width + INNER), BF16, "half"),
            (full, BF16, "row hbm"),
            (full, BF16, "row hbm"),
            (state_shape, BF16, "row"),
        ],
        [wide, wide],
        cost(2e9, 8e6),
    )
    ce_sum = Sum(ce)
    hidden = jnp.concatenate([h_fwd[0], h_rc[0]], axis=0)
    hidden_theirs = their_half(hidden)

    entering = jnp.zeros(state_shape, F32)
    early, early_got = None, None
    for bit in range(bits):
        last = bit == bits - 1
        send = to_send(d_state, bit, last)
        if bit == 1:
            send, early.send, ce_sum.array = together(send, early.send, ce_sum.array)
        elif bit > 1:
            send, ce_sum.array = together(send, ce_sum.array)
        theirs = partner(send, "ctx", bit)
        if bit == 1:
            early_got = partner(early.send, "ctx", 0)
        if bit > 0:
            ce_sum.step()
        else:
            early = RowShare([nsum, hidden], [their_half(nsum), hidden_theirs], d_cot)
            theirs, early.send = together(theirs, early.send)
        if last:
            early.pass_on(early_got)
            theirs, early.send = together(theirs, early.send)
            early_got = partner(early.send, "ctx", early.bit)
        d_state, entering = scan_round(d_state, entering, bit, last, rounds[bit], theirs)
    following = entering.astype(BF16)
    d_val, d_key, d_read, d_a, d_dt = call(
        adjoint_kernel,
        "adjoint",
        [
            (proj, "row hbm"),
            (carry, "row"),
            (d_left, "row hbm"),
            (d_right, "row hbm"),
            (bias, "all"),
            (alog, "all"),
            (skip, "all"),
        ],
        [
            (full, BF16, "row"),
            ((rows, length, STATE), F32, "row"),
            ((rows, length, STATE), F32, "row"),
            ((rows, length, HEADS), F32, "row"),
            ((rows, length, HEADS), F32, "row"),
        ],
        [((HEADS, length), F32), ((HEADS, length), F32), wide, wide],
        cost(8e9, 6e6),
    )
    (d_rest,) = call(
        finish_kernel,
        "finish",
        [
            (proj, "row hbm"),
            (carry, "row"),
            (following, "row"),
            (d_val, "row"),
            (d_key, "row"),
            (d_read, "row"),
            (d_a, "row"),
            (d_dt, "row"),
            (bias, "all"),
            (alog, "all"),
        ],
        [((flat, REST), BF16, "half")],
        [wide, wide],
        cost(2e9, 5e6),
    )
    late = RowShare([hidden], [hidden_theirs], d_rest)
    late.send, d_rest = together(late.send, d_rest)
    grad_fwd, grad_rc = call(
        input_kernel,
        "input",
        [(d_rest, "half"), (d_cot, "half"), (win_t, "all")],
        [(h_fwd.shape, BF16, "all"), (h_rc.shape, BF16, "all")],
        (),
        cost(2e9, 7e6),
    )
    while not late.done():
        first = late.bit == 0
        late.send, ce_sum.array = together(late.send, ce_sum.array)
        late_got = partner(late.send, "ctx", late.bit)
        ce_sum.step()
        if first:
            late_got, grad_fwd, grad_rc = together(late_got, grad_fwd, grad_rc)
        if not early.done():
            late_got, early_got = together(late_got, early_got)
        late.pass_on(late_got)
        if not early.done():
            early.pass_on(early_got)
            if not early.done():
                late.send, early.send = together(late.send, early.send)
                early_got = partner(early.send, "ctx", early.bit)
    ce_sums = ce_sum.finish()[0, :kinds]
    grad_w_in = jnp.concatenate(
        [late.mine[:, :INNER], early.mine[:, width:], late.mine[:, INNER:USED]], axis=1
    )
    scaled = jnp.exp(-log_var) / jnp.maximum((counts + their_counts)[0, 0, :kinds], 1.0)
    loss = jnp.sum(scaled * ce_sums + log_var).reshape(1)
    grad_log_var = 1.0 - scaled * ce_sums
    return (loss, grad_log_var, grad_fwd, grad_rc, grad_w_in, early.mine[:, :width])


def solution(mesh):
    return jax.shard_map(
        on_device,
        mesh=mesh,
        in_specs=(
            P(("groups", "dp"), "ctx", None),
            P(("groups", "dp"), "ctx", None),
            P(("groups", "dp"), "ctx"),
            P(("groups", "dp"), "ctx"),
            P(("groups", "dp")),
            P(),
            P(),
            P(),
            P(),
            P(),
            P(),
            P(),
            P(),
            P(),
        ),
        out_specs=(
            P("groups"),
            P("groups"),
            P(("groups", "dp"), "ctx", None),
            P(("groups", "dp"), "ctx", None),
            P(("groups", "dp", "ctx"), None),
            P(("groups", "dp", "ctx"), None),
        ),
        check_vma=False,
    )
```
